256 devices in a mesh: gz: 8 (over x, core), gy: 32 (over y, z).
Axes of the slice: x: 4, y: 4, z: 8, core: 2. Of those that a mesh axis runs over, the one named last changes fastest.
Arguments:
- zone_ids: int32 [64, 1024, 512], P('gz', 'gy'), may hold values from 0 to 7
- fixed_cells: int32 [64, 1024, 512], P('gz', 'gy'), may hold values 0 or 1
- pressure_old: float32 [64, 1024, 512], P('gz', 'gy'), may hold values from -6 to 6
- pressure_iter: float32 [64, 1024, 512], P('gz', 'gy'), may hold values from -6 to 6
- strain_change: float32 [64, 1024, 512], P('gz', 'gy'), may hold values from -3 to 3
- source: float32 [64, 1024, 512], P('gz', 'gy'), may hold values from -40 to 40
- zone_perm: float32 [8], replicated, may hold values from 0.2 to 5
- zone_storage: float32 [8], replicated, may hold values from 0.1 to 1
- zone_biot: float32 [8], replicated, may hold values from 0.5 to 1
- zone_bulk: float32 [8], replicated, may hold values from 0.5 to 2
Outputs:
- pressure: float32 [64, 1024, 512], P('gz', 'gy')
- strain_next: float32 [64, 1024, 512], P('gz', 'gy')
- outer_norms: float32 [2], replicated
The draws below stay inside these ranges and needn't reach their ends.
All inputs are finite; a program needn't handle non-finite values. No bound on the sum of `fixed_cells` on one device may be relied on, other than what follows from the above.
Results may differ from the reference program's by a relative error of at most 0.00016.
Values sent between devices are 32-bit elements; how exact they have to be, the bound alone decides.
A program may use at most 64 MiB of HBM per device.

```python
import math
import jax
import jax.numpy as jnp

NX = 512
ITERS = 3
ZONES = 8
NZ = 64
NY = 1024
CELLS = 33554432


def draw_source(key, part):
    rough_key = jax.random.fold_in(jax.random.fold_in(key, 17), 0)
    z_position = (jnp.arange(NZ, dtype=jnp.float32) / max(NZ - 1, 1))[:, None, None]
    y_position = (jnp.arange(NY, dtype=jnp.float32) / max(NY - 1, 1))[None, :, None]
    ramp_scale = 1.0 + z_position + y_position
    rough_part = jax.random.truncated_normal(rough_key, -4.0, 4.0, (NZ, NY, NX), jnp.float32)
    return rough_part * ramp_scale


def touch_ends(entries, stream_key, low, largest):
    place = [jax.random.randint(jax.random.fold_in(stream_key, axis), (), 0, length) for axis, length in enumerate(entries.shape)]
    main_axis = entries.shape.index(max(entries.shape))
    beside = place[:main_axis] + [(place[main_axis] + 1) % entries.shape[main_axis]] + place[main_axis + 1:]
    return entries.at[tuple(place)].set(low).at[tuple(beside)].set(largest)


def block_levels(key, extent, cuts, least, largest):
    loudness, own = 1.0, jax.random.fold_in(key, 6)
    for position, parts in cuts:
        steps = jnp.exp(jax.random.uniform(jax.random.fold_in(own, position), (parts,), jnp.float32, least / len(cuts), largest / len(cuts)))
        loudness = loudness * jnp.repeat(steps, extent[position] // parts).reshape([-1 if axis == position else 1 for axis in range(len(extent))])
    return loudness


def normal_values(key, dims, deviation, bound, shards=(), kind=jnp.bfloat16):
    entries = jax.random.normal(key, dims, jnp.float32) * deviation
    if len(shards) > 0:
        entries = block_levels(key, dims, shards, -0.22, 0.18) * entries
    return jnp.clip(entries, min=-bound, max=bound).astype(kind)


def setup_inputs(seed: int = 0) -> dict:
    key_of = jax.random.split(jax.random.key(seed), 11)
    return {
        "zone_ids": touch_ends(jax.random.randint(key_of[0], (NZ, NY, NX), 0, ZONES), jax.random.fold_in(key_of[0], 1), 0, ZONES - 1).astype(jnp.int32),
        "fixed_cells": touch_ends((jax.random.randint(key_of[1], (NZ, NY, NX), 0, 16) < 1).astype(jnp.int32), jax.random.fold_in(key_of[1], 1), 0, 1),
        "pressure_old": normal_values(key_of[2], (NZ, NY, NX), 1.0, 6.0, ((0, 8), (1, 32)), jnp.float32),
        "pressure_iter": normal_values(key_of[3], (NZ, NY, NX), 1.0, 6.0, ((0, 8), (1, 32)), jnp.float32),
        "strain_change": normal_values(key_of[4], (NZ, NY, NX), 0.5, 3.0, ((0, 8), (1, 32)), jnp.float32),
        "source": draw_source(jax.random.fold_in(key_of[10], 71), 0),
        "zone_perm": jnp.clip(jnp.exp(jax.random.uniform(key_of[6], (ZONES,), jnp.float32, math.log(0.2), math.log(5.0))), 0.2, 5.0),
        "zone_storage": jnp.clip(jnp.exp(jax.random.uniform(key_of[7], (ZONES,), jnp.float32, math.log(0.1), math.log(1.0))), 0.1, 1.0),
        "zone_biot": jnp.clip(jax.random.uniform(key_of[8], (ZONES,), jnp.float32, 0.5, 1.0), 0.5, 1.0),
        "zone_bulk": jnp.clip(jnp.exp(jax.random.uniform(key_of[9], (ZONES,), jnp.float32, math.log(0.5), math.log(2.0))), 0.5, 2.0),
    }


def lookup(zone_ids, zone_table):
    result = jnp.zeros(zone_ids.shape, jnp.float32)
    for zone_index in range(zone_table.shape[0]):
        result = jnp.where(zone_ids == zone_index, zone_table[zone_index], result)
    return result

def harmonic(lower_side, upper_side):
    return 2.0 * lower_side * upper_side / (lower_side + upper_side)

def neighbour_views(padded):
    return (padded[:-2, 1:-1, 1:-1], padded[2:, 1:-1, 1:-1], padded[1:-1, :-2, 1:-1], padded[1:-1, 2:, 1:-1], padded[1:-1, 1:-1, :-2], padded[1:-1, 1:-1, 2:])

def reference(zone_ids, fixed_cells, pressure_old, pressure_iter, strain_change, source, zone_perm, zone_storage, zone_biot, zone_bulk):
    storage = lookup(zone_ids, zone_storage)
    biot_coeff = lookup(zone_ids, zone_biot)
    bulk_modulus = lookup(zone_ids, zone_bulk)
    permeability = lookup(zone_ids, zone_perm)
    coupling = biot_coeff * biot_coeff / bulk_modulus
    face_terms = tuple((harmonic(permeability, view) for view in neighbour_views(jnp.pad(permeability, 1))))
    diagonal = storage + coupling
    for face in face_terms:
        diagonal = diagonal + face
    free_cells = 1.0 - fixed_cells.astype(jnp.float32)

    def operator(values):
        views = neighbour_views(jnp.pad(values, 1))
        neighbours = face_terms[0] * views[0]
        for number in range(1, 6):
            neighbours = neighbours + face_terms[number] * views[number]
        return diagonal * values - neighbours
    right_side = storage * pressure_old + coupling * pressure_iter - biot_coeff * strain_change + source
    pressure = pressure_iter
    residual = free_cells * (right_side - operator(pressure_iter))
    precond = residual / diagonal
    direction = precond
    inner_now = jnp.sum(residual * precond)
    for step_index in range(ITERS):
        applied = free_cells * operator(direction)
        step_size = inner_now / jnp.sum(direction * applied)
        pressure = pressure + step_size * direction
        residual = residual - step_size * applied
        if step_index + 1 < ITERS:
            precond = residual / diagonal
            inner_next = jnp.sum(residual * precond)
            direction = precond + inner_next / inner_now * direction
            inner_now = inner_next
    change = biot_coeff / bulk_modulus * (pressure - pressure_iter)
    strain_next = strain_change + change
    closing = free_cells * (right_side - operator(pressure))
    outer_norms = jnp.sqrt(jnp.stack([jnp.sum(closing * closing), jnp.sum(change * change)]) / CELLS)
    return (pressure, strain_next, outer_norms)
```

```python
import jax
import jax.numpy as jnp
from jax import lax
from jax.experimental import pallas as pl
from jax.experimental.pallas import tpu as pltpu
from jax.sharding import PartitionSpec as P

MESH = pl.DeviceIdType.MESH
F32 = jnp.float32
CORES = 2
LINE = 8
LANES = 128
HALO = 3
TOP = 8
SUMS = 24


def halo_box(side_z, side_y, depth_z, depth_y, nz, ny):
    def one(side, depth, base, size):
        if side == 0:
            return base, base, size
        if side > 0:
            return base, base + size, depth
        return base + size - depth, base - depth, depth

    sz, dz, lz = one(side_z, depth_z, HALO, nz)
    sy, dy, ly = one(side_y, depth_y, TOP, ny)
    src = (pl.ds(sz, lz), slice(None), pl.ds(sy, ly))
    dst = (pl.ds(dz, lz), slice(None), pl.ds(dy, ly))
    return src, dst


FACES = ((-1, 0), (1, 0), (0, -1), (0, 1))
CORNERS = ((-1, -1), (-1, 1), (1, -1), (1, 1))


def pick(zone, table):
    b0 = (zone & 1) != 0
    b1 = (zone & 2) != 0
    b2 = (zone & 4) != 0

    def one(t):
        low = [jnp.where(b0, t[2 * i + 1], t[2 * i]) for i in range(4)]
        mid = [jnp.where(b1, low[2 * i + 1], low[2 * i]) for i in range(2)]
        return jnp.where(b2, mid[1], mid[0])

    return [one(t) for t in table]


def harmonic(a, b):
    return 2.0 * a * b / jnp.maximum(a + b, 1e-20)


def body(shape_z, shape_y, nz, ny, nt, zone_hbm, fixed_hbm, old_hbm, iter_hbm, strain_hbm,
         source_hbm, perm_s, stor_s, biot_s, bulk_s, press_out, strain_out, norms_out,
         zb, fb, pb, kb, fx, fy, fz, cb, u0, u1, u2, db, gb, bb, ob, sb, qb,
         partial, slots_a, mid, slots_b,
         lsem, ssem, rsem, asem, arsem, bsem, brsem):
    gz = lax.axis_index("gz")
    gy = lax.axis_index("gy")
    chips = shape_z // CORES
    rows_y = shape_y // LINE
    my_x, my_core = gz // CORES, gz % CORES
    my_y, my_z = gy // LINE, gy % LINE

    def near(side_z, side_y):
        return ((gz - side_z + shape_z) % shape_z, (gy - side_y + shape_y) % shape_y)

    size_a = LINE * CORES
    size_b = chips * rows_y
    rank_a = my_z * CORES + my_core
    rank_b = my_y * chips + my_x

    def peer_a(rank):
        return (my_x * CORES + rank % CORES, my_y * LINE + rank // CORES)

    def peer_b(rank):
        return (rank % chips * CORES + my_core, rank // chips * LINE + my_z)

    barrier = pltpu.get_barrier_semaphore()
    for j in range(1, size_a):
        pl.semaphore_signal(barrier, inc=1, device_id=peer_a((rank_a + j) % size_a), device_id_type=MESH)
    for j in range(1, size_b):
        pl.semaphore_signal(barrier, inc=1, device_id=peer_b((rank_b + j) % size_b), device_id_type=MESH)
    for side in FACES + CORNERS:
        pl.semaphore_signal(barrier, inc=1, device_id=near(*side), device_id_type=MESH)

    loads = []
    for n, (src, dst, ext) in enumerate((
        (zone_hbm, zb, True), (iter_hbm, pb, True), (fixed_hbm, fb, True),
        (old_hbm, ob, False), (strain_hbm, sb, False), (source_hbm, qb, False),
    )):
        group = []
        for t in range(nt):
            view = src.at[:, :, pl.ds(LANES * t, LANES)]
            if ext:
                into = dst.at[pl.ds(HALO, nz), t, pl.ds(TOP, ny), :]
            else:
                into = dst.at[:, t]
            copy = pltpu.make_async_copy(view, into, lsem.at[n, t])
            copy.start()
            group.append(copy)
        loads.append(group)

    for group in loads[:3]:
        for copy in group:
            copy.wait()
    pl.semaphore_wait(barrier, size_a - 1 + size_b - 1 + len(FACES) + len(CORNERS))

    counter = [0]

    def send(ref, side, depth_z, depth_y):
        src, dst = halo_box(side[0], side[1], depth_z, depth_y, nz, ny)
        i = counter[0]
        counter[0] += 1
        copy = pltpu.make_async_remote_copy(
            src_ref=ref.at[src], dst_ref=ref.at[dst], send_sem=ssem.at[i], recv_sem=rsem.at[i],
            device_id=near(*side), device_id_type=MESH)
        copy.start()
        return copy

    first = [send(pb, side, 1, 1) for side in FACES]
    first += [send(zb, side, 3, 3) for side in FACES]
    first += [send(zb, side, 2, 2) for side in CORNERS]
    later = [send(fb, side, 2, 2) for side in FACES]
    later += [send(fb, side, 1, 1) for side in CORNERS]

    for group in loads[3:]:
        for copy in group:
            copy.wait()

    perm = [perm_s[i] for i in range(8)]
    stor = [stor_s[i] for i in range(8)]
    biot = [biot_s[i] for i in range(8)]
    gain = [biot_s[i] / bulk_s[i] for i in range(8)]
    coup = [biot[i] * biot[i] / bulk_s[i] for i in range(8)]
    keep = [stor[i] + coup[i] for i in range(8)]

    lane = lax.broadcasted_iota(jnp.int32, (8, LANES), 1)
    own = pl.ds(TOP, ny)

    @pl.loop(0, nz)
    def _(z):
        for t in range(nt):
            s, a, c, g, k = pick(zb[z + HALO, t, own, :], (stor, biot, coup, gain, perm))
            kb[z + HALO, t, own, :] = k
            gb[z, t] = g
            db[z, t] = s + c
            bb[z, t] = s * ob[z, t] + c * pb[z + HALO, t, own, :] - a * sb[z, t] + qb[z, t]

    for copy in first:
        copy.wait()

    has_lo, has_hi = gz > 0, gz < shape_z - 1
    has_below, has_above = gy > 0, gy < shape_y - 1

    def put_perm(z, start, size, live):
        row = lax.broadcasted_iota(jnp.int32, (size, LANES), 0) + start
        inside = ((row >= TOP) | has_below) & ((row < TOP + ny) | has_above) & live
        for t in range(nt):
            (k,) = pick(zb[z, t, pl.ds(start, size), :], (perm,))
            kb[z, t, pl.ds(start, size), :] = jnp.where(inside, k, 0.0)

    for z in range(HALO):
        put_perm(z, 0, 48, has_lo)
        put_perm(z + HALO + nz, 0, 48, has_hi)

    @pl.loop(HALO, HALO + nz)
    def _(z):
        put_perm(z, 0, 8, gz >= 0)
        put_perm(z, TOP + ny, 8, gz >= 0)

    def x_up(tiles, wrap):
        rolled = [pltpu.roll(v, LANES - 1, 1) for v in tiles]
        last = lax.broadcasted_iota(jnp.int32, tiles[0].shape, 1) == LANES - 1
        out = []
        for t in range(nt):
            nxt = rolled[t + 1] if t + 1 < nt else (rolled[0] if wrap else jnp.zeros_like(rolled[0]))
            out.append(jnp.where(last, nxt, rolled[t]))
        return out

    def x_down(tiles):
        rolled = [pltpu.roll(v, 1, 1) for v in tiles]
        head = lax.broadcasted_iota(jnp.int32, tiles[0].shape, 1) == 0
        return [jnp.where(head, rolled[t - 1], rolled[t]) for t in range(nt)]

    def put_faces_x(z, start, size):
        rows = pl.ds(start, size)
        k = [kb[z, t, rows, :] for t in range(nt)]
        up = x_up(k, False)
        for t in range(nt):
            fx[z, t, rows, :] = harmonic(k[t], up[t])

    def put_faces_y(z, start, size):
        for t in range(nt):
            fy[z, t, pl.ds(start, size), :] = harmonic(
                kb[z, t, pl.ds(start, size), :], kb[z, t, pl.ds(start + 1, size), :])

    def put_faces_z(z, start, size):
        for t in range(nt):
            fz[z, t, pl.ds(start, size), :] = harmonic(
                kb[z, t, pl.ds(start, size), :], kb[z + 1, t, pl.ds(start, size), :])

    def diagonal(base, z, start, size):
        rows = pl.ds(start, size)
        low_x = x_down([fx[z, t, rows, :] for t in range(nt)])
        out = []
        for t in range(nt):
            d = base[t] + fz[z - 1, t, rows, :] + fz[z, t, rows, :]
            d = d + fy[z, t, pl.ds(start - 1, size), :] + fy[z, t, rows, :]
            out.append(d + low_x[t] + fx[z, t, rows, :])
        return out

    def around(src, z, start, size):
        rows, under, over = pl.ds(start, size), pl.ds(start - 1, size), pl.ds(start + 1, size)
        mid_v = [src[z, t, rows, :] for t in range(nt)]
        face = [fx[z, t, rows, :] for t in range(nt)]
        up = x_up(mid_v, True)
        down = x_down([face[t] * mid_v[t] for t in range(nt)])
        out = []
        for t in range(nt):
            total = fz[z - 1, t, rows, :] * src[z - 1, t, rows, :] + fz[z, t, rows, :] * src[z + 1, t, rows, :]
            total = total + fy[z, t, under, :] * src[z, t, under, :] + fy[z, t, rows, :] * src[z, t, over, :]
            out.append(total + down[t] + face[t] * up[t])
        return out

    put_faces_z(HALO - 1, TOP, ny)

    @pl.loop(HALO, HALO + nz)
    def _(z):
        put_faces_z(z, TOP, ny)
        put_faces_y(z, 7, 40)
        put_faces_x(z, TOP, ny)

    @pl.loop(0, nz)
    def _(z):
        zz = z + HALO
        diag = diagonal([db[z, t] for t in range(nt)], zz, TOP, ny)
        near_sum = around(pb, zz, TOP, ny)
        for t in range(nt):
            d = diag[t]
            free = 1.0 - fb[zz, t, own, :].astype(F32)
            c = free / d
            db[z, t] = d
            cb[zz, t, own, :] = c
            u0[zz, t, own, :] = c * (bb[z, t] - (d * pb[zz, t, own, :] - near_sum[t]))

    second = [send(u0, side, 3, 3) for side in FACES]
    second += [send(u0, side, 2, 2) for side in CORNERS]

    for copy in later:
        copy.wait()

    def put_scale(z, start, size):
        rows = pl.ds(start, size)
        base = [pick(zb[z, t, rows, :], (keep,))[0] for t in range(nt)]
        diag = diagonal(base, z, start, size)
        for t in range(nt):
            cb[z, t, rows, :] = (1.0 - fb[z, t, rows, :].astype(F32)) / diag[t]

    put_faces_z(0, 5, 40)
    for z in (1, 2, HALO + nz, HALO + nz + 1):
        put_faces_z(z, 5, 40)
        put_faces_y(z, 5, 40)
        put_faces_x(z, 5, 40)

    @pl.loop(HALO, HALO + nz)
    def _(z):
        for start in (0, 39):
            put_faces_z(z, start, 8)
            put_faces_y(z, start, 8)
            put_faces_x(z, start, 8)

    for z in (1, 2, HALO + nz, HALO + nz + 1):
        put_scale(z, 6, 40)

    @pl.loop(HALO, HALO + nz)
    def _(z):
        for start in (1, 39):
            put_scale(z, start, 8)

    for copy in second:
        copy.wait()

    @pl.loop(1, HALO + nz + 2)
    def _(z):
        new = around(u0, z, 6, 40)
        for t in range(nt):
            u1[z, t, pl.ds(6, 40), :] = cb[z, t, pl.ds(6, 40), :] * new[t]

    @pl.loop(2, HALO + nz + 1)
    def _(z):
        new = around(u1, z, 7, 40)
        for t in range(nt):
            u2[z, t, pl.ds(7, 40), :] = cb[z, t, pl.ds(7, 40), :] * new[t]

    def fold(v):
        total = v[0:8]
        for i in range(8, v.shape[0], 8):
            total = total + v[i:i + 8]
        return total

    def gram_step(z, acc):
        zz = z + HALO
        new = around(u2, zz, TOP, ny)
        acc = list(acc)
        for t in range(nt):
            d, g = db[z, t], gb[z, t]
            u = [u0[zz, t, own, :], u1[zz, t, own, :], u2[zz, t, own, :]]
            free = 1.0 - fb[zz, t, own, :].astype(F32)
            w = [d * v for v in u] + [free * new[t]]
            s = [g * v for v in u]
            e = 0
            for i, j in ((0, 0), (0, 1), (1, 1), (1, 2), (2, 2), (2, 3)):
                acc[e] = acc[e] + fold(u[i] * w[j])
                e += 1
            for i in range(4):
                for j in range(i, 4):
                    acc[e] = acc[e] + fold(w[i] * w[j])
                    e += 1
            for i in range(3):
                for j in range(i, 3):
                    acc[e] = acc[e] + fold(s[i] * s[j])
                    e += 1
        return tuple(acc)

    zero = jnp.zeros((8, LANES), F32)
    acc = list(lax.fori_loop(0, nz, gram_step, (zero,) * 22))
    acc += [zero] * (SUMS - len(acc))

    sub = lax.broadcasted_iota(jnp.int32, (8, LANES), 0)

    def merge(a, b, step):
        take = (sub & step) == 0
        return jnp.where(take, a, b) + pltpu.roll(jnp.where(take, b, a), step, 0)

    line = jnp.zeros((8, LANES), F32)
    for i in range(SUMS // 8):
        rows8 = acc[8 * i:8 * i + 8]
        four = [merge(rows8[j], rows8[j + 1], 1) for j in range(0, 8, 2)]
        two = [merge(four[j], four[j + 1], 2) for j in range(0, 4, 2)]
        one = merge(two[0], two[1], 4)
        whole = jnp.sum(one, axis=1, keepdims=True)
        line = line + jnp.where(lane == sub + 8 * i, whole, 0.0)
    mine = jnp.sum(line, axis=0, keepdims=True)

    def all_sum(value, source, slots, rank, size, peer, out_sem, in_sem):
        source[...] = value
        slots[rank] = value
        copies = []
        for j in range(1, size):
            to = (rank + j) % size
            copy = pltpu.make_async_remote_copy(
                src_ref=source, dst_ref=slots.at[rank], send_sem=out_sem.at[j], recv_sem=in_sem.at[j],
                device_id=peer(to), device_id_type=MESH)
            copy.start()
            copies.append(copy)
        for copy in copies:
            copy.wait()
        total = slots[0]
        for j in range(1, size):
            total = total + slots[j]
        return total

    total = all_sum(mine, partial, slots_a, rank_a, size_a, peer_a, asem, arsem)
    total = all_sum(total, mid, slots_b, rank_b, size_b, peer_b, bsem, brsem)

    def at(e):
        return jnp.broadcast_to(total[:, e:e + 1], (1, LANES))

    m = [at(e) for e in range(6)]
    h = [m[i] - m[i + 1] for i in range(5)]
    l1, l2 = h[1] / h[0], h[2] / h[0]
    d1 = h[2] - l1 * h[1]
    e1 = h[3] - l1 * h[2]
    y1 = m[1] - l1 * m[0]
    ok1 = d1 > 1e-7 * h[2]
    safe1 = jnp.where(ok1, d1, 1.0)
    l3 = e1 / safe1
    d2 = h[4] - l2 * h[2] - l3 * e1
    y2 = m[2] - l2 * m[0] - l3 * y1
    ok2 = ok1 & (d2 > 1e-7 * h[4])
    c2 = jnp.where(ok2, y2 / jnp.where(ok2, d2, 1.0), 0.0)
    c1 = jnp.where(ok1, (y1 - e1 * c2) / safe1, 0.0)
    c0 = (m[0] - h[1] * c1 - h[2] * c2) / h[0]

    rest = [1.0 - c0, c0 - c1, c1 - c2, c2]
    coef = [c0, c1, c2]
    e = 6
    closing = jnp.zeros((1, LANES), F32)
    for i in range(4):
        for j in range(i, 4):
            closing = closing + (1.0 if i == j else 2.0) * rest[i] * rest[j] * at(e)
            e += 1
    moved = jnp.zeros((1, LANES), F32)
    for i in range(3):
        for j in range(i, 3):
            moved = moved + (1.0 if i == j else 2.0) * coef[i] * coef[j] * at(e)
            e += 1
    cells = float(nz * shape_z * ny * shape_y * nt * LANES)
    norms_out[...] = jnp.sqrt(jnp.maximum(jnp.where(lane[0:1] == 0, closing, moved), 0.0) / cells)

    b0, b1, b2 = [jnp.broadcast_to(v, (ny, LANES)) for v in coef]

    @pl.loop(0, nz)
    def _(z):
        zz = z + HALO
        for t in range(nt):
            delta = b0 * u0[zz, t, own, :] + b1 * u1[zz, t, own, :] + b2 * u2[zz, t, own, :]
            press_out[z, :, pl.ds(LANES * t, LANES)] = pb[zz, t, own, :] + delta
            strain_out[z, :, pl.ds(LANES * t, LANES)] = sb[z, t] + gb[z, t] * delta


def solution(mesh):
    shape_z, shape_y = mesh.shape["gz"], mesh.shape["gy"]

    def per_device(zone_ids, fixed_cells, pressure_old, pressure_iter, strain_change, source,
                   zone_perm, zone_storage, zone_biot, zone_bulk):
        nz, ny, nx = zone_ids.shape
        nt = nx // LANES
        size_a = LINE * CORES
        size_b = shape_z * shape_y // size_a
        ext = (nz + 2 * HALO, nt, ny + 2 * TOP, LANES)
        inner = (nz, nt, ny, LANES)
        block = jax.ShapeDtypeStruct((nz, ny, nx), F32)
        dma = pltpu.SemaphoreType.DMA

        def kernel(*refs):
            body(shape_z, shape_y, nz, ny, nt, *refs)

        pressure, strain_next, norms = pl.pallas_call(
            kernel,
            out_shape=(block, block, jax.ShapeDtypeStruct((1, LANES), F32)),
            in_specs=[pl.BlockSpec(memory_space=pl.ANY)] * 6 + [pl.BlockSpec(memory_space=pltpu.SMEM)] * 4,
            out_specs=tuple([pl.BlockSpec(memory_space=pltpu.VMEM)] * 3),
            scratch_shapes=[
                pltpu.VMEM(ext, jnp.int32), pltpu.VMEM(ext, jnp.int32),
            ] + [pltpu.VMEM(ext, F32)] * 9 + [pltpu.VMEM(inner, F32)] * 6 + [
                pltpu.VMEM((1, LANES), F32), pltpu.VMEM((size_a, 1, LANES), F32),
                pltpu.VMEM((1, LANES), F32), pltpu.VMEM((size_b, 1, LANES), F32),
                dma((6, nt)), dma((32,)), dma((32,)),
                dma((size_a,)), dma((size_a,)), dma((size_b,)), dma((size_b,)),
            ],
            compiler_params=pltpu.CompilerParams(collective_id=0, has_side_effects=True),
        )(zone_ids, fixed_cells, pressure_old, pressure_iter, strain_change, source,
          zone_perm, zone_storage, zone_biot, zone_bulk)
        return pressure, strain_next, norms[0, :2]

    field = P("gz", "gy", None)
    return jax.shard_map(
        per_device, mesh=mesh,
        in_specs=(field,) * 6 + (P(),) * 4,
        out_specs=(field, field, P()),
        check_vma=False,
    )
```

```python
import jax
import jax.numpy as jnp
from jax import lax
from jax.experimental import pallas as pl
from jax.experimental.pallas import tpu as pltpu
from jax.sharding import PartitionSpec as P

MESH = pl.DeviceIdType.MESH
F32 = jnp.float32
CORES = 2
LINE = 8
LANES = 128
HALO = 3
TOP = 8


def halo_box(side, layers_z, layers_y, nz, ny):
    def one(toward, layers, base, size):
        low, high = layers
        if toward == 0:
            return base, base, size
        if toward > 0:
            return base + low, base + size + low, high - low
        return base + size - high, base - high, high - low

    sz, dz, lz = one(side[0], layers_z, HALO, nz)
    sy, dy, ly = one(side[1], layers_y, TOP, ny)
    src = (pl.ds(sz, lz), slice(None), pl.ds(sy, ly))
    dst = (pl.ds(dz, lz), slice(None), pl.ds(dy, ly))
    return src, dst


FACES_Z = ((-1, 0), (1, 0))
FACES_Y = ((0, -1), (0, 1))
CORNERS = ((-1, -1), (-1, 1), (1, -1), (1, 1))


def pick(zone, table):
    b0 = (zone & 1) != 0
    b1 = (zone & 2) != 0
    b2 = (zone & 4) != 0

    def one(t):
        low = [jnp.where(b0, t[2 * i + 1], t[2 * i]) for i in range(4)]
        mid = [jnp.where(b1, low[2 * i + 1], low[2 * i]) for i in range(2)]
        return jnp.where(b2, mid[1], mid[0])

    return [one(t) for t in table]


def harmonic(a, b):
    return 2.0 * a * b / jnp.maximum(a + b, 1e-20)


def body(shape_z, shape_y, nz, ny, nt, zone_hbm, fixed_hbm, old_hbm, iter_hbm, strain_hbm,
         source_hbm, perm_s, stor_s, biot_s, bulk_s, press_out, strain_out, norms_out,
         zb, fb, pb, kb, fx, fy, fz, cb, u0, u1, u2, db, gb, bb, ob, sb, qb, eb, w3,
         lines, slots_a1, slots_b1, slots_a2, slots_b2,
         lsem, ssem, rsem, asem, arsem, bsem, brsem):
    gz = lax.axis_index("gz")
    gy = lax.axis_index("gy")
    chips = shape_z // CORES
    rows_y = shape_y // LINE
    my_x, my_core = gz // CORES, gz % CORES
    my_y, my_z = gy // LINE, gy % LINE
    has = {-1: (gz > 0, gy > 0), 0: (gz >= 0, gy >= 0), 1: (gz < shape_z - 1, gy < shape_y - 1)}

    def exists(side):
        return has[side[0]][0] & has[side[1]][1]

    def opposite(side):
        return (-side[0], -side[1])

    size_a = LINE * CORES
    size_b = chips * rows_y
    rank_a = my_z * CORES + my_core
    rank_b = my_y * chips + my_x

    def peer_a(rank):
        return (my_x * CORES + rank % CORES, my_y * LINE + rank // CORES)

    def peer_b(rank):
        return (rank % chips * CORES + my_core, rank // chips * LINE + my_z)

    barrier = pltpu.get_barrier_semaphore()
    expected = size_a - 1 + size_b - 1
    for side in FACES_Y + FACES_Z + CORNERS:
        expected = expected + jnp.where(exists(side), 1, 0)

        @pl.when(exists(side))
        def _():
            pl.semaphore_signal(barrier, inc=1, device_id=(gz + side[0], gy + side[1]), device_id_type=MESH)
    for j in range(1, size_a):
        pl.semaphore_signal(barrier, inc=1, device_id=peer_a((rank_a + j) % size_a), device_id_type=MESH)
    for j in range(1, size_b):
        pl.semaphore_signal(barrier, inc=1, device_id=peer_b((rank_b + j) % size_b), device_id_type=MESH)

    loads = []
    for n, (src, dst, ext) in enumerate((
        (zone_hbm, zb, True), (iter_hbm, pb, True), (fixed_hbm, fb, True),
        (old_hbm, ob, False), (strain_hbm, sb, False), (source_hbm, qb, False),
    )):
        group = []
        for t in range(nt):
            view = src.at[:, :, pl.ds(LANES * t, LANES)]
            if ext:
                into = dst.at[pl.ds(HALO, nz), t, pl.ds(TOP, ny), :]
            else:
                into = dst.at[:, t]
            copy = pltpu.make_async_copy(view, into, lsem.at[n, t])
            copy.start()
            group.append(copy)
        loads.append(group)

    own = pl.ds(TOP, ny)
    far = HALO + nz

    def clear_planes(z0):
        for t in range(nt):
            for z in range(z0, z0 + HALO):
                u0[z, t] = jnp.zeros(u0.shape[2:], F32)
                pb[z, t] = jnp.zeros(pb.shape[2:], F32)

    def clear_rows(start):
        @pl.loop(0, nz + 2 * HALO)
        def _(z):
            for t in range(nt):
                u0[z, t, pl.ds(start, TOP), :] = jnp.zeros((TOP, LANES), F32)
                pb[z, t, pl.ds(start, TOP), :] = jnp.zeros((TOP, LANES), F32)

    @pl.when(gz == 0)
    def _():
        clear_planes(0)

    @pl.when(gz == shape_z - 1)
    def _():
        clear_planes(far)

    @pl.when(gy == 0)
    def _():
        clear_rows(0)

    @pl.when(gy == shape_y - 1)
    def _():
        clear_rows(TOP + ny)

    for group in loads[:2]:
        for copy in group:
            copy.wait()
    pl.semaphore_wait(barrier, expected)

    counter = [0]
    sent = []

    def send(side, parts):
        copies = []
        for ref, layers_z, layers_y in parts:
            src, dst = halo_box(side, layers_z, layers_y, nz, ny)
            i = counter[0]
            counter[0] += 1
            copies.append(pltpu.make_async_remote_copy(
                src_ref=ref.at[src], dst_ref=ref.at[dst], send_sem=ssem.at[i], recv_sem=rsem.at[i],
                device_id=(gz - side[0], gy - side[1]), device_id_type=MESH))

        @pl.when(exists(opposite(side)))
        def _():
            for copy in copies:
                copy.start()
        sent.append((side, copies))
        return side, copies

    def receive(group):
        for side, copies in group:
            @pl.when(exists(side))
            def _():
                for copy in copies:
                    copy.wait_recv()

    one, rest, two, three = (0, 1), (1, 3), (0, 2), (0, 3)
    first = [send(side, ((pb, one, one), (zb, one, one))) for side in FACES_Y + FACES_Z]
    for copy in loads[2]:
        copy.wait()
    later = [send(side, ((zb, two, two), (fb, one, one))) for side in CORNERS]
    later += [send(side, ((zb, rest, rest), (fb, two, two))) for side in FACES_Y + FACES_Z]

    for group in loads[3:]:
        for copy in group:
            copy.wait()

    perm = [perm_s[i] for i in range(8)]
    stor = [stor_s[i] for i in range(8)]
    biot = [biot_s[i] for i in range(8)]
    gain = [biot_s[i] / bulk_s[i] for i in range(8)]
    coup = [biot[i] * biot[i] / bulk_s[i] for i in range(8)]
    keep = [stor[i] + coup[i] for i in range(8)]

    lane = lax.broadcasted_iota(jnp.int32, (8, LANES), 1)

    def x_up(tiles, wrap):
        rolled = [pltpu.roll(v, LANES - 1, 1) for v in tiles]
        last = lax.broadcasted_iota(jnp.int32, tiles[0].shape, 1) == LANES - 1
        out = []
        for t in range(nt):
            nxt = rolled[t + 1] if t + 1 < nt else (rolled[0] if wrap else jnp.zeros_like(rolled[0]))
            out.append(jnp.where(last, nxt, rolled[t]))
        return out

    def x_down(tiles):
        rolled = [pltpu.roll(v, 1, 1) for v in tiles]
        head = lax.broadcasted_iota(jnp.int32, tiles[0].shape, 1) == 0
        return [jnp.where(head, rolled[t - 1], rolled[t]) for t in range(nt)]

    def put_faces_x(z, start, size):
        rows = pl.ds(start, size)
        k = [kb[z, t, rows, :] for t in range(nt)]
        up = x_up(k, False)
        for t in range(nt):
            fx[z, t, rows, :] = harmonic(k[t], up[t])

    def put_faces_y(z, start, size):
        for t in range(nt):
            fy[z, t, pl.ds(start, size), :] = harmonic(
                kb[z, t, pl.ds(start, size), :], kb[z, t, pl.ds(start + 1, size), :])

    def put_faces_z(z, start, size):
        for t in range(nt):
            fz[z, t, pl.ds(start, size), :] = harmonic(
                kb[z, t, pl.ds(start, size), :], kb[z + 1, t, pl.ds(start, size), :])

    def diagonal(base, z, start, size):
        rows = pl.ds(start, size)
        low_x = x_down([fx[z, t, rows, :] for t in range(nt)])
        out = []
        for t in range(nt):
            d = base[t] + fz[z - 1, t, rows, :] + fz[z, t, rows, :]
            d = d + fy[z, t, pl.ds(start - 1, size), :] + fy[z, t, rows, :]
            out.append(d + low_x[t] + fx[z, t, rows, :])
        return out

    def around(src, z, start, size):
        rows, under, over = pl.ds(start, size), pl.ds(start - 1, size), pl.ds(start + 1, size)
        mid_v = [src[z, t, rows, :] for t in range(nt)]
        face = [fx[z, t, rows, :] for t in range(nt)]
        up = x_up(mid_v, True)
        down = x_down([face[t] * mid_v[t] for t in range(nt)])
        out = []
        for t in range(nt):
            total = fz[z - 1, t, rows, :] * src[z - 1, t, rows, :] + fz[z, t, rows, :] * src[z + 1, t, rows, :]
            total = total + fy[z, t, under, :] * src[z, t, under, :] + fy[z, t, rows, :] * src[z, t, over, :]
            out.append(total + down[t] + face[t] * up[t])
        return out

    def begin(z, start, size):
        rows, inner = pl.ds(start, size), pl.ds(start - TOP, size)
        diag = diagonal([eb[z - HALO, t, inner, :] for t in range(nt)], z, start, size)
        near_sum = around(pb, z, start, size)
        for t in range(nt):
            d = diag[t]
            c = (1.0 - fb[z, t, rows, :].astype(F32)) / d
            db[z - HALO, t, inner, :] = d
            cb[z, t, rows, :] = c
            u0[z, t, rows, :] = c * (bb[z - HALO, t, inner, :] - (d * pb[z, t, rows, :] - near_sum[t]))

    def advance(src, dst, z, start, size):
        rows = pl.ds(start, size)
        new = around(src, z, start, size)
        for t in range(nt):
            dst[z, t, rows, :] = cb[z, t, rows, :] * new[t]

    @pl.loop(0, nz)
    def _(z):
        for t in range(nt):
            s, a, c, g, k = pick(zb[z + HALO, t, own, :], (stor, biot, coup, gain, perm))
            kb[z + HALO, t, own, :] = k
            gb[z, t] = g
            eb[z, t] = s + c
            bb[z, t] = s * ob[z, t] + c * pb[z + HALO, t, own, :] - a * sb[z, t] + qb[z, t]

    @pl.loop(HALO, far)
    def _(z):
        put_faces_y(z, TOP, ny - 1)
        put_faces_x(z, TOP, ny)

    @pl.loop(HALO, far - 1)
    def _(z):
        put_faces_z(z, TOP, ny)

    @pl.loop(HALO + 1, far - 1)
    def _(z):
        begin(z, TOP + 1, ny - 2)

    receive(first)

    def put_perm(z, start, size, live):
        row = lax.broadcasted_iota(jnp.int32, (size, LANES), 0) + start
        inside = ((row >= TOP) | has[-1][1]) & ((row < TOP + ny) | has[1][1]) & live
        for t in range(nt):
            (k,) = pick(zb[z, t, pl.ds(start, size), :], (perm,))
            kb[z, t, pl.ds(start, size), :] = jnp.where(inside, k, 0.0)

    put_perm(HALO - 1, TOP, ny, has[-1][0])
    put_perm(far, TOP, ny, has[1][0])
    put_faces_z(HALO - 1, TOP, ny)
    put_faces_z(far - 1, TOP, ny)

    @pl.loop(HALO, far)
    def _(z):
        put_perm(z, TOP - 1, 1, has[0][0])
        put_perm(z, TOP + ny, 1, has[0][0])
        put_faces_y(z, TOP - 1, 1)
        put_faces_y(z, TOP + ny - 1, 1)

    begin(HALO, TOP, ny)
    begin(far - 1, TOP, ny)

    @pl.loop(HALO + 1, far - 1)
    def _(z):
        begin(z, TOP, 1)
        begin(z, TOP + ny - 1, 1)

    second_corners = [send(side, ((u0, two, two),)) for side in CORNERS]
    second = [send(side, ((u0, three, three),)) for side in FACES_Y + FACES_Z]

    @pl.loop(HALO + 1, far - 1)
    def _(z):
        advance(u0, u1, z, TOP + 1, ny - 2)

    receive(later)

    def put_scale(z, start, size):
        rows = pl.ds(start, size)
        base = [pick(zb[z, t, rows, :], (keep,))[0] for t in range(nt)]
        diag = diagonal(base, z, start, size)
        for t in range(nt):
            cb[z, t, rows, :] = (1.0 - fb[z, t, rows, :].astype(F32)) / diag[t]

    for z in range(HALO):
        put_perm(z, 5, 40, has[-1][0])
        put_perm(far + z, 5, 40, has[1][0])

    @pl.loop(HALO, far)
    def _(z):
        put_perm(z, 5, 3, has[0][0])
        put_perm(z, TOP + ny, 3, has[0][0])

    put_faces_z(0, 5, 40)
    for z in (1, 2, far, far + 1):
        put_faces_z(z, 5, 40)
        put_faces_y(z, 5, 38)
        put_faces_x(z, 5, 40)

    @pl.loop(HALO, far)
    def _(z):
        for start in (6, 40):
            put_faces_z(z, start, 2)
            put_faces_x(z, start, 2)
        put_faces_y(z, 5, 2)
        put_faces_y(z, 40, 2)

    for z in (1, 2, far, far + 1):
        put_scale(z, 6, 36)

    @pl.loop(HALO, far)
    def _(z):
        put_scale(z, 6, 2)
        put_scale(z, 40, 2)

    receive(second)
    receive(second_corners)

    @pl.loop(HALO + 1, far - 1)
    def _(z):
        advance(u0, u1, z, 6, 3)
        advance(u0, u1, z, 39, 3)
    for z in (HALO, far - 1):
        advance(u0, u1, z, 6, 36)
    for z in (HALO - 1, far):
        advance(u0, u1, z, 7, 34)
    for z in (HALO - 2, far + 1):
        advance(u0, u1, z, 8, 32)

    advance(u1, u2, HALO - 1, TOP, ny)
    advance(u1, u2, far, TOP, ny)

    @pl.loop(HALO, far)
    def _(z):
        advance(u1, u2, z, TOP - 1, ny + 2)

    def fold(v):
        total = v[0:8]
        for i in range(8, v.shape[0], 8):
            total = total + v[i:i + 8]
        return total

    def moment_step(z, acc):
        zz = z + HALO
        new = around(u2, zz, TOP, ny)
        acc = list(acc)
        for t in range(nt):
            d = db[z, t]
            last = (1.0 - fb[zz, t, own, :].astype(F32)) * new[t]
            w3[z, t] = last
            u = [u0[zz, t, own, :], u1[zz, t, own, :], u2[zz, t, own, :]]
            w = [d * v for v in u] + [last]
            for e, (i, j) in enumerate(((0, 0), (0, 1), (1, 1), (1, 2), (2, 2), (2, 3))):
                acc[e] = acc[e] + fold(u[i] * w[j])
        return tuple(acc)

    def norm_step(z, acc):
        zz = z + HALO
        acc = list(acc)
        for t in range(nt):
            d, g = db[z, t], gb[z, t]
            u = [u0[zz, t, own, :], u1[zz, t, own, :], u2[zz, t, own, :]]
            w = [d * v for v in u] + [w3[z, t]]
            s = [g * v for v in u]
            e = 0
            for i in range(4):
                for j in range(i, 4):
                    acc[e] = acc[e] + fold(w[i] * w[j])
                    e += 1
            for i in range(3):
                for j in range(i, 3):
                    acc[e] = acc[e] + fold(s[i] * s[j])
                    e += 1
        return tuple(acc)

    sub = lax.broadcasted_iota(jnp.int32, (8, LANES), 0)
    zero = jnp.zeros((8, LANES), F32)

    def merge(a, b, step):
        take = (sub & step) == 0
        return jnp.where(take, a, b) + pltpu.roll(jnp.where(take, b, a), step, 0)

    def in_lanes(acc):
        line = zero
        for i in range(0, len(acc), 8):
            eight = (acc[i:i + 8] + [zero] * 8)[:8]
            four = [merge(eight[j], eight[j + 1], 1) for j in range(0, 8, 2)]
            pair = [merge(four[j], four[j + 1], 2) for j in range(0, 4, 2)]
            whole = jnp.sum(merge(pair[0], pair[1], 4), axis=1, keepdims=True)
            line = line + jnp.where(lane == sub + i, whole, 0.0)
        return jnp.sum(line, axis=0, keepdims=True)

    def share(value, place, slots, rank, size, peer, out_sem, in_sem):
        lines[place] = value
        slots[rank] = value
        copies = []
        for j in range(1, size):
            copy = pltpu.make_async_remote_copy(
                src_ref=lines.at[place], dst_ref=slots.at[rank], send_sem=out_sem.at[j], recv_sem=in_sem.at[j],
                device_id=peer((rank + j) % size), device_id_type=MESH)
            copy.start()
            copies.append(copy)
        return copies

    def gather(copies, slots, size):
        for copy in copies:
            copy.wait_recv()
        total = [slots[j] for j in range(size)]
        while len(total) > 1:
            total = [total[j] + total[j + 1] for j in range(0, len(total), 2)]
        return total[0]

    acc = list(lax.fori_loop(0, nz, moment_step, (zero,) * 6))
    flight_a1 = share(in_lanes(acc), 0, slots_a1, rank_a, size_a, peer_a, asem.at[0], arsem.at[0])
    acc = list(lax.fori_loop(0, nz, norm_step, (zero,) * 16))
    flight_a2 = share(in_lanes(acc), 1, slots_a2, rank_a, size_a, peer_a, asem.at[1], arsem.at[1])
    part = gather(flight_a1, slots_a1, size_a)
    flight_b1 = share(part, 2, slots_b1, rank_b, size_b, peer_b, bsem.at[0], brsem.at[0])
    part = gather(flight_a2, slots_a2, size_a)
    flight_b2 = share(part, 3, slots_b2, rank_b, size_b, peer_b, bsem.at[1], brsem.at[1])
    total = gather(flight_b1, slots_b1, size_b)

    def at(e):
        return jnp.broadcast_to(total[:, e:e + 1], (1, LANES))

    m = [at(e) for e in range(6)]
    h = [m[i] - m[i + 1] for i in range(5)]
    l1, l2 = h[1] / h[0], h[2] / h[0]
    d1 = h[2] - l1 * h[1]
    e1 = h[3] - l1 * h[2]
    y1 = m[1] - l1 * m[0]
    ok1 = d1 > 1e-7 * h[2]
    safe1 = jnp.where(ok1, d1, 1.0)
    l3 = e1 / safe1
    d2 = h[4] - l2 * h[2] - l3 * e1
    y2 = m[2] - l2 * m[0] - l3 * y1
    ok2 = ok1 & (d2 > 1e-7 * h[4])
    c2 = jnp.where(ok2, y2 / jnp.where(ok2, d2, 1.0), 0.0)
    c1 = jnp.where(ok1, (y1 - e1 * c2) / safe1, 0.0)
    c0 = (m[0] - h[1] * c1 - h[2] * c2) / h[0]
    coef = [c0, c1, c2]

    b0, b1, b2 = [jnp.broadcast_to(v, (ny, LANES)) for v in coef]

    @pl.loop(0, nz)
    def _(z):
        zz = z + HALO
        for t in range(nt):
            delta = b0 * u0[zz, t, own, :] + b1 * u1[zz, t, own, :] + b2 * u2[zz, t, own, :]
            press_out[z, t] = pb[zz, t, own, :] + delta
            strain_out[z, t] = sb[z, t] + gb[z, t] * delta

    total = gather(flight_b2, slots_b2, size_b)
    left = [1.0 - c0, c0 - c1, c1 - c2, c2]
    e = 0
    closing = jnp.zeros((1, LANES), F32)
    for i in range(4):
        for j in range(i, 4):
            closing = closing + (1.0 if i == j else 2.0) * left[i] * left[j] * at(e)
            e += 1
    moved = jnp.zeros((1, LANES), F32)
    for i in range(3):
        for j in range(i, 3):
            moved = moved + (1.0 if i == j else 2.0) * coef[i] * coef[j] * at(e)
            e += 1
    cells = float(nz * shape_z * ny * shape_y * nt * LANES)
    norms_out[...] = jnp.sqrt(jnp.maximum(jnp.where(lane[0:1] == 0, closing, moved), 0.0) / cells)

    for side, copies in sent:
        @pl.when(exists(opposite(side)))
        def _():
            for copy in copies:
                copy.wait_send()
    for copy in flight_a1 + flight_a2 + flight_b1 + flight_b2:
        copy.wait_send()


def solution(mesh):
    shape_z, shape_y = mesh.shape["gz"], mesh.shape["gy"]

    def per_device(zone_ids, fixed_cells, pressure_old, pressure_iter, strain_change, source,
                   zone_perm, zone_storage, zone_biot, zone_bulk):
        nz, ny, nx = zone_ids.shape
        nt = nx // LANES
        size_a = LINE * CORES
        size_b = shape_z * shape_y // size_a
        ext = (nz + 2 * HALO, nt, ny + 2 * TOP, LANES)
        inner = (nz, nt, ny, LANES)
        block = jax.ShapeDtypeStruct((nz, ny, nx), F32)
        dma = pltpu.SemaphoreType.DMA

        def kernel(*refs):
            body(shape_z, shape_y, nz, ny, nt, *refs)

        results = pl.pallas_call(
            kernel,
            out_shape=(pltpu.VMEM(inner, F32), pltpu.VMEM(inner, F32), pltpu.VMEM((1, LANES), F32)),
            in_specs=[pl.BlockSpec(memory_space=pl.ANY)] * 6 + [pl.BlockSpec(memory_space=pltpu.SMEM)] * 4,
            out_specs=tuple([pl.BlockSpec(memory_space=pltpu.VMEM)] * 3),
            scratch_shapes=[
                pltpu.VMEM(ext, jnp.int32), pltpu.VMEM(ext, jnp.int32),
            ] + [pltpu.VMEM(ext, F32)] * 9 + [pltpu.VMEM(inner, F32)] * 8 + [
                pltpu.VMEM((4, 1, LANES), F32),
                pltpu.VMEM((size_a, 1, LANES), F32), pltpu.VMEM((size_b, 1, LANES), F32),
                pltpu.VMEM((size_a, 1, LANES), F32), pltpu.VMEM((size_b, 1, LANES), F32),
                dma((6, nt)), dma((40,)), dma((40,)),
                dma((2, size_a)), dma((2, size_a)), dma((2, size_b)), dma((2, size_b)),
            ],
            compiler_params=pltpu.CompilerParams(collective_id=0, has_side_effects=True),
        )(zone_ids, fixed_cells, pressure_old, pressure_iter, strain_change, source,
          zone_perm, zone_storage, zone_biot, zone_bulk)

        def emit(press_in, strain_in, norms_in, press_ref, strain_ref, norms_ref, sem):
            copies = []
            for i, (a, b) in enumerate(((press_in, press_ref), (strain_in, strain_ref))):
                for t in range(nt):
                    copy = pltpu.make_async_copy(a.at[:, t], b.at[:, :, pl.ds(LANES * t, LANES)], sem.at[i, t])
                    copy.start()
                    copies.append(copy)
            norms_ref[0] = norms_in[0, 0]
            norms_ref[1] = norms_in[0, 1]
            for copy in copies:
                copy.wait()

        return pl.pallas_call(
            emit,
            out_shape=(block, block, jax.ShapeDtypeStruct((2,), F32)),
            in_specs=[pl.BlockSpec(memory_space=pltpu.VMEM)] * 3,
            out_specs=(pl.BlockSpec(memory_space=pl.ANY),) * 2 + (pl.BlockSpec(memory_space=pltpu.SMEM),),
            scratch_shapes=[dma((2, nt))],
        )(*[pltpu.with_memory_space_constraint(v, pltpu.VMEM) for v in results])

    field = P("gz", "gy", None)
    return jax.shard_map(
        per_device, mesh=mesh,
        in_specs=(field,) * 6 + (P(),) * 4,
        out_specs=(field, field, P()),
        check_vma=False,
    )
```

```python
import jax
import jax.numpy as jnp
from jax import lax
from jax.experimental import pallas as pl
from jax.experimental.pallas import tpu as pltpu
from jax.sharding import PartitionSpec as P

MESH = pl.DeviceIdType.MESH
F32 = jnp.float32
CORES = 2
LINE = 8
LANES = 128
HALO = 3
TOP = 8


def halo_box(side, layers_z, layers_y, nz, ny):
    def one(toward, layers, base, size):
        low, high = layers
        if toward == 0:
            return base, base, size
        if toward > 0:
            return base + low, base + size + low, high - low
        return base + size - high, base - high, high - low

    sz, dz, lz = one(side[0], layers_z, HALO, nz)
    sy, dy, ly = one(side[1], layers_y, TOP, ny)
    src = (pl.ds(sz, lz), slice(None), pl.ds(sy, ly))
    dst = (pl.ds(dz, lz), slice(None), pl.ds(dy, ly))
    return src, dst


FACES_Z = ((-1, 0), (1, 0))
FACES_Y = ((0, -1), (0, 1))
CORNERS = ((-1, -1), (-1, 1), (1, -1), (1, 1))


def pick(zone, table):
    b0 = (zone & 1) != 0
    b1 = (zone & 2) != 0
    b2 = (zone & 4) != 0

    def one(t):
        low = [jnp.where(b0, t[2 * i + 1], t[2 * i]) for i in range(4)]
        mid = [jnp.where(b1, low[2 * i + 1], low[2 * i]) for i in range(2)]
        return jnp.where(b2, mid[1], mid[0])

    return [one(t) for t in table]


def harmonic(a, b):
    return 2.0 * a * b / jnp.maximum(a + b, 1e-20)


def body(shape_z, shape_y, nz, ny, nt, zone_hbm, fixed_hbm, old_hbm, iter_hbm, strain_hbm,
         source_hbm, perm_hbm, stor_hbm, biot_hbm, bulk_hbm, press_out, strain_out, tail_out,
         zb, fb, pb, kb, fx, fy, fz, cb, u0, u1, u2, db, gb, bb, ob, sb, qb, eb, w3,
         perm_s, stor_s, biot_s, bulk_s, lines, slots_a1, slots_b1, slots_a2, slots_b2,
         tsem, lsem, ssem, rsem, asem, arsem, bsem, brsem):
    gz = lax.axis_index("gz")
    gy = lax.axis_index("gy")
    chips = shape_z // CORES
    rows_y = shape_y // LINE
    my_x, my_core = gz // CORES, gz % CORES
    my_y, my_z = gy // LINE, gy % LINE
    has = {-1: (gz > 0, gy > 0), 0: (gz >= 0, gy >= 0), 1: (gz < shape_z - 1, gy < shape_y - 1)}

    def exists(side):
        return has[side[0]][0] & has[side[1]][1]

    def opposite(side):
        return (-side[0], -side[1])

    size_a = LINE * CORES
    size_b = chips * rows_y
    rank_a = my_z * CORES + my_core
    rank_b = my_y * chips + my_x

    def wrap(value, size):
        return jnp.where(value >= size, value - size, value)

    def peer_a(j):
        return (my_x * CORES + wrap(my_core + j % CORES, CORES), my_y * LINE + wrap(my_z + j // CORES, LINE))

    def peer_b(j):
        return (wrap(my_x + j % chips, chips) * CORES + my_core, wrap(my_y + j // chips, rows_y) * LINE + my_z)

    barrier = pltpu.get_barrier_semaphore()
    for j in range(1, size_a):
        pl.semaphore_signal(barrier, inc=1, device_id=peer_a(j), device_id_type=MESH)
    for j in range(1, size_b):
        pl.semaphore_signal(barrier, inc=1, device_id=peer_b(j), device_id_type=MESH)
    expected = size_a - 1 + size_b - 1
    for side in CORNERS + FACES_Y + FACES_Z:
        expected = expected + jnp.where(exists(side), 1, 0)

        @pl.when(exists(side))
        def _():
            pl.semaphore_signal(barrier, inc=1, device_id=(gz + side[0], gy + side[1]), device_id_type=MESH)

    loads = []
    for n, (src, dst, ext) in enumerate((
        (zone_hbm, zb, True), (iter_hbm, pb, True), (fixed_hbm, fb, True),
        (old_hbm, ob, False), (strain_hbm, sb, False), (source_hbm, qb, False),
    )):
        group = []
        for t in range(nt):
            view = src.at[:, :, pl.ds(LANES * t, LANES)]
            if ext:
                into = dst.at[pl.ds(HALO, nz), t, pl.ds(TOP, ny), :]
            else:
                into = dst.at[:, t]
            copy = pltpu.make_async_copy(view, into, lsem.at[n, t])
            copy.start()
            group.append(copy)
        loads.append(group)

    tables = []
    for i, (src, dst) in enumerate(((perm_hbm, perm_s), (stor_hbm, stor_s), (biot_hbm, biot_s), (bulk_hbm, bulk_s))):
        copy = pltpu.make_async_copy(src, dst, tsem.at[i])
        copy.start()
        tables.append(copy)

    own = pl.ds(TOP, ny)
    far = HALO + nz

    def clear_planes(z0):
        for t in range(nt):
            for z in range(z0, z0 + HALO):
                u0[z, t] = jnp.zeros(u0.shape[2:], F32)
                pb[z, t] = jnp.zeros(pb.shape[2:], F32)

    def clear_rows(start):
        @pl.loop(0, nz + 2 * HALO)
        def _(z):
            for t in range(nt):
                u0[z, t, pl.ds(start, TOP), :] = jnp.zeros((TOP, LANES), F32)
                pb[z, t, pl.ds(start, TOP), :] = jnp.zeros((TOP, LANES), F32)

    @pl.when(gz == 0)
    def _():
        clear_planes(0)

    @pl.when(gz == shape_z - 1)
    def _():
        clear_planes(far)

    @pl.when(gy == 0)
    def _():
        clear_rows(0)

    @pl.when(gy == shape_y - 1)
    def _():
        clear_rows(TOP + ny)

    for group in loads[:2]:
        for copy in group:
            copy.wait()
    pl.semaphore_wait(barrier, expected)

    counter = [0]
    sent = []

    def send(side, parts):
        copies = []
        for ref, layers_z, layers_y in parts:
            src, dst = halo_box(side, layers_z, layers_y, nz, ny)
            i = counter[0]
            counter[0] += 1
            copies.append(pltpu.make_async_remote_copy(
                src_ref=ref.at[src], dst_ref=ref.at[dst], send_sem=ssem.at[i], recv_sem=rsem.at[i],
                device_id=(gz - side[0], gy - side[1]), device_id_type=MESH))

        @pl.when(exists(opposite(side)))
        def _():
            for copy in copies:
                copy.start()
        sent.append((side, copies))
        return side, copies

    def receive(group):
        for side, copies in group:
            @pl.when(exists(side))
            def _():
                for copy in copies:
                    copy.wait_recv()

    one, rest, two, three = (0, 1), (1, 3), (0, 2), (0, 3)
    first_y = [send(side, ((pb, one, one), (zb, one, one))) for side in FACES_Y]
    first_z = [send(side, ((pb, one, one), (zb, one, one))) for side in FACES_Z]
    for copy in loads[2]:
        copy.wait()
    later = [send(side, ((zb, two, two), (fb, one, one))) for side in CORNERS]
    later += [send(side, ((zb, rest, rest), (fb, two, two))) for side in FACES_Y + FACES_Z]

    for group in loads[3:]:
        for copy in group:
            copy.wait()

    for copy in tables:
        copy.wait()
    perm = [perm_s[i] for i in range(8)]
    stor = [stor_s[i] for i in range(8)]
    biot = [biot_s[i] for i in range(8)]
    gain = [biot_s[i] / bulk_s[i] for i in range(8)]
    coup = [biot[i] * biot[i] / bulk_s[i] for i in range(8)]
    keep = [stor[i] + coup[i] for i in range(8)]

    lane = lax.broadcasted_iota(jnp.int32, (8, LANES), 1)

    def x_up(tiles, wrap):
        rolled = [pltpu.roll(v, LANES - 1, 1) for v in tiles]
        last = lax.broadcasted_iota(jnp.int32, tiles[0].shape, 1) == LANES - 1
        out = []
        for t in range(nt):
            nxt = rolled[t + 1] if t + 1 < nt else (rolled[0] if wrap else jnp.zeros_like(rolled[0]))
            out.append(jnp.where(last, nxt, rolled[t]))
        return out

    def x_down(tiles):
        rolled = [pltpu.roll(v, 1, 1) for v in tiles]
        head = lax.broadcasted_iota(jnp.int32, tiles[0].shape, 1) == 0
        return [jnp.where(head, rolled[t - 1], rolled[t]) for t in range(nt)]

    def put_faces_x(z, start, size):
        rows = pl.ds(start, size)
        k = [kb[z, t, rows, :] for t in range(nt)]
        up = x_up(k, False)
        for t in range(nt):
            fx[z, t, rows, :] = harmonic(k[t], up[t])

    def put_faces_y(z, start, size):
        for t in range(nt):
            fy[z, t, pl.ds(start, size), :] = harmonic(
                kb[z, t, pl.ds(start, size), :], kb[z, t, pl.ds(start + 1, size), :])

    def put_faces_z(z, start, size):
        for t in range(nt):
            fz[z, t, pl.ds(start, size), :] = harmonic(
                kb[z, t, pl.ds(start, size), :], kb[z + 1, t, pl.ds(start, size), :])

    def diagonal(base, z, start, size):
        rows = pl.ds(start, size)
        low_x = x_down([fx[z, t, rows, :] for t in range(nt)])
        out = []
        for t in range(nt):
            d = base[t] + fz[z - 1, t, rows, :] + fz[z, t, rows, :]
            d = d + fy[z, t, pl.ds(start - 1, size), :] + fy[z, t, rows, :]
            out.append(d + low_x[t] + fx[z, t, rows, :])
        return out

    def around(src, z, start, size):
        rows, under, over = pl.ds(start, size), pl.ds(start - 1, size), pl.ds(start + 1, size)
        mid_v = [src[z, t, rows, :] for t in range(nt)]
        face = [fx[z, t, rows, :] for t in range(nt)]
        up = x_up(mid_v, True)
        down = x_down([face[t] * mid_v[t] for t in range(nt)])
        out = []
        for t in range(nt):
            total = fz[z - 1, t, rows, :] * src[z - 1, t, rows, :] + fz[z, t, rows, :] * src[z + 1, t, rows, :]
            total = total + fy[z, t, under, :] * src[z, t, under, :] + fy[z, t, rows, :] * src[z, t, over, :]
            out.append(total + down[t] + face[t] * up[t])
        return out

    def begin(z, start, size):
        rows, inner = pl.ds(start, size), pl.ds(start - TOP, size)
        diag = diagonal([eb[z - HALO, t, inner, :] for t in range(nt)], z, start, size)
        near_sum = around(pb, z, start, size)
        for t in range(nt):
            d = diag[t]
            c = (1.0 - fb[z, t, rows, :].astype(F32)) / d
            db[z - HALO, t, inner, :] = d
            cb[z, t, rows, :] = c
            u0[z, t, rows, :] = c * (bb[z - HALO, t, inner, :] - (d * pb[z, t, rows, :] - near_sum[t]))

    def advance(src, dst, z, start, size):
        rows = pl.ds(start, size)
        new = around(src, z, start, size)
        for t in range(nt):
            dst[z, t, rows, :] = cb[z, t, rows, :] * new[t]

    @pl.loop(0, nz)
    def _(z):
        for t in range(nt):
            s, a, c, g, k = pick(zb[z + HALO, t, own, :], (stor, biot, coup, gain, perm))
            kb[z + HALO, t, own, :] = k
            gb[z, t] = g
            eb[z, t] = s + c
            bb[z, t] = s * ob[z, t] + c * pb[z + HALO, t, own, :] - a * sb[z, t] + qb[z, t]

    @pl.loop(HALO, far)
    def _(z):
        put_faces_y(z, TOP, ny - 1)
        put_faces_x(z, TOP, ny)

    @pl.loop(HALO, far - 1)
    def _(z):
        put_faces_z(z, TOP, ny)

    @pl.loop(HALO + 1, far - 1)
    def _(z):
        begin(z, TOP + 1, ny - 2)

    receive(first_z)

    def put_perm(z, start, size, live):
        row = lax.broadcasted_iota(jnp.int32, (size, LANES), 0) + start
        inside = ((row >= TOP) | has[-1][1]) & ((row < TOP + ny) | has[1][1]) & live
        for t in range(nt):
            (k,) = pick(zb[z, t, pl.ds(start, size), :], (perm,))
            kb[z, t, pl.ds(start, size), :] = jnp.where(inside, k, 0.0)

    put_perm(HALO - 1, TOP, ny, has[-1][0])
    put_perm(far, TOP, ny, has[1][0])
    put_faces_z(HALO - 1, TOP, ny)
    put_faces_z(far - 1, TOP, ny)

    begin(HALO, TOP + 1, ny - 2)
    begin(far - 1, TOP + 1, ny - 2)
    receive(first_y)

    @pl.loop(HALO, far)
    def _(z):
        put_perm(z, TOP - 1, 1, has[0][0])
        put_perm(z, TOP + ny, 1, has[0][0])
        put_faces_y(z, TOP - 1, 1)
        put_faces_y(z, TOP + ny - 1, 1)
        begin(z, TOP, 1)
        begin(z, TOP + ny - 1, 1)

    second_corners = [send(side, ((u0, two, two),)) for side in CORNERS]
    second = [send(side, ((u0, three, three),)) for side in FACES_Y + FACES_Z]

    @pl.loop(HALO + 1, far - 1)
    def _(z):
        advance(u0, u1, z, TOP + 1, ny - 2)

    @pl.loop(HALO + 2, far - 2)
    def _(z):
        advance(u1, u2, z, TOP + 2, ny - 4)

    receive(later)

    def put_scale(z, start, size):
        rows = pl.ds(start, size)
        base = [pick(zb[z, t, rows, :], (keep,))[0] for t in range(nt)]
        diag = diagonal(base, z, start, size)
        for t in range(nt):
            cb[z, t, rows, :] = (1.0 - fb[z, t, rows, :].astype(F32)) / diag[t]

    for z in range(HALO):
        put_perm(z, 5, 40, has[-1][0])
        put_perm(far + z, 5, 40, has[1][0])

    @pl.loop(HALO, far)
    def _(z):
        put_perm(z, 5, 3, has[0][0])
        put_perm(z, TOP + ny, 3, has[0][0])

    put_faces_z(0, 5, 40)
    for z in (1, 2, far, far + 1):
        put_faces_z(z, 5, 40)
        put_faces_y(z, 5, 38)
        put_faces_x(z, 5, 40)

    @pl.loop(HALO, far)
    def _(z):
        for start in (6, 40):
            put_faces_z(z, start, 2)
            put_faces_x(z, start, 2)
        put_faces_y(z, 5, 2)
        put_faces_y(z, 40, 2)

    for z in (1, 2, far, far + 1):
        put_scale(z, 6, 36)

    @pl.loop(HALO, far)
    def _(z):
        put_scale(z, 6, 2)
        put_scale(z, 40, 2)

    receive(second)
    receive(second_corners)

    @pl.loop(HALO + 1, far - 1)
    def _(z):
        advance(u0, u1, z, 6, 3)
        advance(u0, u1, z, 39, 3)
    for z in (HALO, far - 1):
        advance(u0, u1, z, 6, 36)
    for z in (HALO - 1, far):
        advance(u0, u1, z, 7, 34)
    for z in (HALO - 2, far + 1):
        advance(u0, u1, z, 8, 32)

    advance(u1, u2, HALO - 1, TOP, ny)
    advance(u1, u2, far, TOP, ny)

    for z in (HALO, HALO + 1, far - 2, far - 1):
        advance(u1, u2, z, TOP - 1, ny + 2)

    @pl.loop(HALO + 2, far - 2)
    def _(z):
        advance(u1, u2, z, TOP - 1, 3)
        advance(u1, u2, z, TOP + ny - 2, 3)

    def fold(v):
        total = v[0:8]
        for i in range(8, v.shape[0], 8):
            total = total + v[i:i + 8]
        return total

    def moment_step(z, acc):
        zz = z + HALO
        new = around(u2, zz, TOP, ny)
        acc = list(acc)
        for t in range(nt):
            d = db[z, t]
            last = (1.0 - fb[zz, t, own, :].astype(F32)) * new[t]
            w3[z, t] = last
            u = [u0[zz, t, own, :], u1[zz, t, own, :], u2[zz, t, own, :]]
            w = [d * v for v in u] + [last]
            for e, (i, j) in enumerate(((0, 0), (0, 1), (1, 1), (1, 2), (2, 2), (2, 3))):
                acc[e] = acc[e] + fold(u[i] * w[j])
        return tuple(acc)

    def norm_step(z, acc):
        zz = z + HALO
        acc = list(acc)
        for t in range(nt):
            d, g = db[z, t], gb[z, t]
            u = [u0[zz, t, own, :], u1[zz, t, own, :], u2[zz, t, own, :]]
            w = [d * v for v in u] + [w3[z, t]]
            s = [g * v for v in u]
            e = 0
            for i in range(4):
                for j in range(i, 4):
                    acc[e] = acc[e] + fold(w[i] * w[j])
                    e += 1
            for i in range(3):
                for j in range(i, 3):
                    acc[e] = acc[e] + fold(s[i] * s[j])
                    e += 1
        return tuple(acc)

    sub = lax.broadcasted_iota(jnp.int32, (8, LANES), 0)
    zero = jnp.zeros((8, LANES), F32)

    def merge(a, b, step):
        take = (sub & step) == 0
        return jnp.where(take, a, b) + pltpu.roll(jnp.where(take, b, a), step, 0)

    def in_lanes(acc):
        line = zero
        for i in range(0, len(acc), 8):
            eight = (acc[i:i + 8] + [zero] * 8)[:8]
            four = [merge(eight[j], eight[j + 1], 1) for j in range(0, 8, 2)]
            pair = [merge(four[j], four[j + 1], 2) for j in range(0, 4, 2)]
            whole = jnp.sum(merge(pair[0], pair[1], 4), axis=1, keepdims=True)
            line = line + jnp.where(lane == sub + i, whole, 0.0)
        return jnp.sum(line, axis=0, keepdims=True)

    def share(value, place, slots, rank, size, peer, out_sem, in_sem):
        lines[place] = value
        slots[rank] = value
        copies = []
        for j in range(1, size):
            copy = pltpu.make_async_remote_copy(
                src_ref=lines.at[place], dst_ref=slots.at[rank], send_sem=out_sem.at[j], recv_sem=in_sem.at[j],
                device_id=peer(j), device_id_type=MESH)
            copy.start()
            copies.append(copy)
        return copies

    def gather(copies, slots, size):
        for copy in copies:
            copy.wait_recv()
        total = [slots[j] for j in range(size)]
        while len(total) > 1:
            total = [total[j] + total[j + 1] for j in range(0, len(total), 2)]
        return total[0]

    acc = list(lax.fori_loop(0, nz, moment_step, (zero,) * 6))
    flight_a1 = share(in_lanes(acc), 0, slots_a1, rank_a, size_a, peer_a, asem.at[0], arsem.at[0])
    acc = list(lax.fori_loop(0, nz, norm_step, (zero,) * 16))
    flight_a2 = share(in_lanes(acc), 1, slots_a2, rank_a, size_a, peer_a, asem.at[1], arsem.at[1])
    for side, copies in sent:
        @pl.when(exists(opposite(side)))
        def _():
            for copy in copies:
                copy.wait_send()
    part = gather(flight_a1, slots_a1, size_a)
    flight_b1 = share(part, 2, slots_b1, rank_b, size_b, peer_b, bsem.at[0], brsem.at[0])
    part = gather(flight_a2, slots_a2, size_a)
    flight_b2 = share(part, 3, slots_b2, rank_b, size_b, peer_b, bsem.at[1], brsem.at[1])
    for copy in flight_a1 + flight_a2:
        copy.wait_send()
    total = gather(flight_b1, slots_b1, size_b)

    def at(e):
        return jnp.broadcast_to(total[:, e:e + 1], (1, LANES))

    m = [at(e) for e in range(6)]
    h = [m[i] - m[i + 1] for i in range(5)]
    l1, l2 = h[1] / h[0], h[2] / h[0]
    d1 = h[2] - l1 * h[1]
    e1 = h[3] - l1 * h[2]
    y1 = m[1] - l1 * m[0]
    ok1 = d1 > 1e-7 * h[2]
    safe1 = jnp.where(ok1, d1, 1.0)
    l3 = e1 / safe1
    d2 = h[4] - l2 * h[2] - l3 * e1
    y2 = m[2] - l2 * m[0] - l3 * y1
    ok2 = ok1 & (d2 > 1e-7 * h[4])
    c2 = jnp.where(ok2, y2 / jnp.where(ok2, d2, 1.0), 0.0)
    c1 = jnp.where(ok1, (y1 - e1 * c2) / safe1, 0.0)
    c0 = (m[0] - h[1] * c1 - h[2] * c2) / h[0]
    coef = [c0, c1, c2]

    b0, b1, b2 = [jnp.broadcast_to(v, (ny, LANES)) for v in coef]

    @pl.loop(0, nz)
    def _(z):
        zz = z + HALO
        for t in range(nt):
            delta = b0 * u0[zz, t, own, :] + b1 * u1[zz, t, own, :] + b2 * u2[zz, t, own, :]
            press_out[z, :, pl.ds(LANES * t, LANES)] = pb[zz, t, own, :] + delta
            strain_out[z, :, pl.ds(LANES * t, LANES)] = sb[z, t] + gb[z, t] * delta

    for copy in flight_b1 + flight_b2:
        copy.wait_send()
    tail_out[0:1, :] = gather(flight_b2, slots_b2, size_b)
    for i in range(3):
        tail_out[i + 1:i + 2, :] = coef[i]


def norms(tail, cells):
    def at(e):
        return jnp.broadcast_to(tail[0:1, e:e + 1], (1, LANES))

    c = [tail[i:i + 1] for i in range(1, 4)]
    left = [1.0 - c[0], c[0] - c[1], c[1] - c[2], c[2]]
    e = 0
    out = []
    for v in (left, c):
        total = jnp.zeros((1, LANES), F32)
        for i in range(len(v)):
            for j in range(i, len(v)):
                total = total + (1.0 if i == j else 2.0) * v[i] * v[j] * at(e)
                e += 1
        out.append(total)
    lane = lax.broadcasted_iota(jnp.int32, (1, LANES), 1)
    return jnp.sqrt(jnp.maximum(jnp.where(lane == 0, out[0], out[1]), 0.0) / cells)


def solution(mesh):
    shape_z, shape_y = mesh.shape["gz"], mesh.shape["gy"]

    def per_device(zone_ids, fixed_cells, pressure_old, pressure_iter, strain_change, source,
                   zone_perm, zone_storage, zone_biot, zone_bulk):
        nz, ny, nx = zone_ids.shape
        nt = nx // LANES
        size_a = LINE * CORES
        size_b = shape_z * shape_y // size_a
        ext = (nz + 2 * HALO, nt, ny + 2 * TOP, LANES)
        inner = (nz, nt, ny, LANES)
        block = jax.ShapeDtypeStruct((nz, ny, nx), F32)
        dma = pltpu.SemaphoreType.DMA

        def kernel(*refs):
            body(shape_z, shape_y, nz, ny, nt, *refs)

        results = pl.pallas_call(
            kernel,
            out_shape=(pltpu.VMEM((nz, ny, nx), F32), pltpu.VMEM((nz, ny, nx), F32), pltpu.VMEM((8, LANES), F32)),
            in_specs=[pl.BlockSpec(memory_space=pl.ANY)] * 10,
            out_specs=tuple([pl.BlockSpec(memory_space=pltpu.VMEM)] * 3),
            scratch_shapes=[
                pltpu.VMEM(ext, jnp.int32), pltpu.VMEM(ext, jnp.int32),
            ] + [pltpu.VMEM(ext, F32)] * 9 + [pltpu.VMEM(inner, F32)] * 8 + [
                pltpu.SMEM((8,), F32), pltpu.SMEM((8,), F32), pltpu.SMEM((8,), F32), pltpu.SMEM((8,), F32),
                pltpu.VMEM((4, 1, LANES), F32),
                pltpu.VMEM((size_a, 1, LANES), F32), pltpu.VMEM((size_b, 1, LANES), F32),
                pltpu.VMEM((size_a, 1, LANES), F32), pltpu.VMEM((size_b, 1, LANES), F32),
                dma((4,)), dma((6, nt)), dma((40,)), dma((40,)),
                dma((2, size_a)), dma((2, size_a)), dma((2, size_b)), dma((2, size_b)),
            ],
            compiler_params=pltpu.CompilerParams(collective_id=0, has_side_effects=True),
        )(zone_ids, fixed_cells, pressure_old, pressure_iter, strain_change, source,
          zone_perm, zone_storage, zone_biot, zone_bulk)

        cells = float(nz * shape_z * ny * shape_y * nx)

        def emit(press_in, strain_in, tail_in, press_ref, strain_ref, norms_ref, sem):
            copies = []
            for i, (a, b) in enumerate(((press_in, press_ref), (strain_in, strain_ref))):
                for j in range(4):
                    part = pl.ds(j * nz // 4, nz // 4)
                    copy = pltpu.make_async_copy(a.at[part], b.at[part], sem.at[i, j])
                    copy.start()
                    copies.append(copy)
            both = norms(tail_in[...], cells)
            norms_ref[0] = both[0, 0]
            norms_ref[1] = both[0, 1]
            for copy in copies:
                copy.wait()

        return pl.pallas_call(
            emit,
            out_shape=(block, block, jax.ShapeDtypeStruct((2,), F32)),
            in_specs=[pl.BlockSpec(memory_space=pltpu.VMEM)] * 3,
            out_specs=(pl.BlockSpec(memory_space=pl.ANY),) * 2 + (pl.BlockSpec(memory_space=pltpu.SMEM),),
            scratch_shapes=[dma((2, 4))],
        )(*[pltpu.with_memory_space_constraint(v, pltpu.VMEM) for v in results])

    field = P("gz", "gy", None)
    return jax.shard_map(
        per_device, mesh=mesh,
        in_specs=(field,) * 6 + (P(),) * 4,
        out_specs=(field, field, P()),
        check_vma=False,
    )
```

```python
import jax
import jax.numpy as jnp
from jax import lax
from jax.experimental import pallas as pl
from jax.experimental.pallas import tpu as pltpu
from jax.sharding import PartitionSpec as P

MESH = pl.DeviceIdType.MESH
F32 = jnp.float32
CORES = 2
LINE = 8
LANES = 128
HALO = 3
TOP = 8


def halo_box(side, layers_z, layers_y, nz, ny):
    def one(toward, layers, base, size):
        low, high = layers
        if toward == 0:
            return base, base, size
        if toward > 0:
            return base + low, base + size + low, high - low
        return base + size - high, base - high, high - low

    sz, dz, lz = one(side[0], layers_z, HALO, nz)
    sy, dy, ly = one(side[1], layers_y, TOP, ny)
    src = (pl.ds(sz, lz), slice(None), pl.ds(sy, ly))
    dst = (pl.ds(dz, lz), slice(None), pl.ds(dy, ly))
    return src, dst


FACES_Z = ((-1, 0), (1, 0))
FACES_Y = ((0, -1), (0, 1))
CORNERS = ((-1, -1), (-1, 1), (1, -1), (1, 1))


def pick(zone, table):
    b0 = (zone & 1) != 0
    b1 = (zone & 2) != 0
    b2 = (zone & 4) != 0

    def one(t):
        low = [jnp.where(b0, t[2 * i + 1], t[2 * i]) for i in range(4)]
        mid = [jnp.where(b1, low[2 * i + 1], low[2 * i]) for i in range(2)]
        return jnp.where(b2, mid[1], mid[0])

    return [one(t) for t in table]


def harmonic(a, b):
    return 2.0 * a * b / jnp.maximum(a + b, 1e-20)


def body(shape_z, shape_y, nz, ny, nt, zone_hbm, fixed_hbm, old_hbm, iter_hbm, strain_hbm,
         source_hbm, perm_hbm, stor_hbm, biot_hbm, bulk_hbm, press_out, strain_out, tail_out,
         zb, fb, pb, kb, fx, fy, fz, cb, u0, u1, u2, db, gb, bb, ob, sb, qb, eb, w3,
         perm_s, stor_s, biot_s, bulk_s, lines, slots_a1, slots_b1, slots_a2, slots_b2,
         tsem, lsem, ssem, rsem, asem, arsem, bsem, brsem):
    gz = lax.axis_index("gz")
    gy = lax.axis_index("gy")
    chips = shape_z // CORES
    rows_y = shape_y // LINE
    my_x, my_core = gz // CORES, gz % CORES
    my_y, my_z = gy // LINE, gy % LINE
    has = {-1: (gz > 0, gy > 0), 0: (gz >= 0, gy >= 0), 1: (gz < shape_z - 1, gy < shape_y - 1)}

    def exists(side):
        return has[side[0]][0] & has[side[1]][1]

    def opposite(side):
        return (-side[0], -side[1])

    size_a = LINE * CORES
    size_b = chips * rows_y
    rank_a = my_z * CORES + my_core
    rank_b = my_y * chips + my_x

    def wrap(value, size):
        return jnp.where(value >= size, value - size, value)

    def peer_a(j):
        return (my_x * CORES + wrap(my_core + j % CORES, CORES), my_y * LINE + wrap(my_z + j // CORES, LINE))

    def peer_b(j):
        return (wrap(my_x + j % chips, chips) * CORES + my_core, wrap(my_y + j // chips, rows_y) * LINE + my_z)

    barrier = pltpu.get_barrier_semaphore()
    for j in range(1, size_a):
        pl.semaphore_signal(barrier, inc=1, device_id=peer_a(j), device_id_type=MESH)
    for j in range(1, size_b):
        pl.semaphore_signal(barrier, inc=1, device_id=peer_b(j), device_id_type=MESH)
    expected = size_a - 1 + size_b - 1
    for side in CORNERS + FACES_Y + FACES_Z:
        expected = expected + jnp.where(exists(side), 1, 0)

        @pl.when(exists(side))
        def _():
            pl.semaphore_signal(barrier, inc=1, device_id=(gz + side[0], gy + side[1]), device_id_type=MESH)

    loads = []
    for n, (src, dst, ext) in enumerate((
        (zone_hbm, zb, True), (iter_hbm, pb, True), (fixed_hbm, fb, True),
        (old_hbm, ob, False), (strain_hbm, sb, False), (source_hbm, qb, False),
    )):
        for t in range(nt):
            view = src.at[:, :, pl.ds(LANES * t, LANES)]
            if ext:
                into = dst.at[pl.ds(HALO, nz), t, pl.ds(TOP, ny), :]
            else:
                into = dst.at[:, t]
            pltpu.make_async_copy(view, into, lsem.at[n]).start()
        whole = dst.at[pl.ds(HALO, nz), :, pl.ds(TOP, ny), :] if ext else dst
        loads.append([pltpu.make_async_copy(whole, whole, lsem.at[n])])

    tables = []
    for i, (src, dst) in enumerate(((perm_hbm, perm_s), (stor_hbm, stor_s), (biot_hbm, biot_s), (bulk_hbm, bulk_s))):
        copy = pltpu.make_async_copy(src, dst, tsem.at[i])
        copy.start()
        tables.append(copy)

    own = pl.ds(TOP, ny)
    far = HALO + nz

    def clear_planes(z0):
        for t in range(nt):
            for z in range(z0, z0 + HALO):
                u0[z, t] = jnp.zeros(u0.shape[2:], F32)
                pb[z, t] = jnp.zeros(pb.shape[2:], F32)

    def clear_rows(start):
        @pl.loop(0, nz + 2 * HALO)
        def _(z):
            for t in range(nt):
                u0[z, t, pl.ds(start, TOP), :] = jnp.zeros((TOP, LANES), F32)
                pb[z, t, pl.ds(start, TOP), :] = jnp.zeros((TOP, LANES), F32)

    @pl.when(gz == 0)
    def _():
        clear_planes(0)

    @pl.when(gz == shape_z - 1)
    def _():
        clear_planes(far)

    @pl.when(gy == 0)
    def _():
        clear_rows(0)

    @pl.when(gy == shape_y - 1)
    def _():
        clear_rows(TOP + ny)

    for group in loads[:2]:
        for copy in group:
            copy.wait()
    pl.semaphore_wait(barrier, expected)

    counter = [0]
    sent = []

    def send(side, parts):
        copies = []
        for ref, layers_z, layers_y in parts:
            src, dst = halo_box(side, layers_z, layers_y, nz, ny)
            i = counter[0]
            counter[0] += 1
            copies.append(pltpu.make_async_remote_copy(
                src_ref=ref.at[src], dst_ref=ref.at[dst], send_sem=ssem.at[i], recv_sem=rsem.at[i],
                device_id=(gz - side[0], gy - side[1]), device_id_type=MESH))

        @pl.when(exists(opposite(side)))
        def _():
            for copy in copies:
                copy.start()
        sent.append((side, copies))
        return side, copies

    def receive(group):
        for side, copies in group:
            @pl.when(exists(side))
            def _():
                for copy in copies:
                    copy.wait_recv()

    one, rest, two, three = (0, 1), (1, 3), (0, 2), (0, 3)
    first_y = [send(side, ((pb, one, one), (zb, one, one))) for side in FACES_Y]
    first_z = [send(side, ((pb, one, one), (zb, one, one))) for side in FACES_Z]
    for copy in loads[2]:
        copy.wait()
    later = [send(side, ((zb, two, two), (fb, one, one))) for side in CORNERS]
    later += [send(side, ((zb, rest, rest), (fb, two, two))) for side in FACES_Y + FACES_Z]

    for group in loads[3:]:
        for copy in group:
            copy.wait()

    for copy in tables:
        copy.wait()
    perm = [perm_s[i] for i in range(8)]
    stor = [stor_s[i] for i in range(8)]
    biot = [biot_s[i] for i in range(8)]
    gain = [biot_s[i] / bulk_s[i] for i in range(8)]
    coup = [biot[i] * biot[i] / bulk_s[i] for i in range(8)]
    keep = [stor[i] + coup[i] for i in range(8)]

    lane = lax.broadcasted_iota(jnp.int32, (8, LANES), 1)

    def x_up(tiles, wrap):
        rolled = [pltpu.roll(v, LANES - 1, 1) for v in tiles]
        last = lax.broadcasted_iota(jnp.int32, tiles[0].shape, 1) == LANES - 1
        out = []
        for t in range(nt):
            nxt = rolled[t + 1] if t + 1 < nt else (rolled[0] if wrap else jnp.zeros_like(rolled[0]))
            out.append(jnp.where(last, nxt, rolled[t]))
        return out

    def x_down(tiles):
        rolled = [pltpu.roll(v, 1, 1) for v in tiles]
        head = lax.broadcasted_iota(jnp.int32, tiles[0].shape, 1) == 0
        return [jnp.where(head, rolled[t - 1], rolled[t]) for t in range(nt)]

    def put_faces_x(z, start, size):
        rows = pl.ds(start, size)
        k = [kb[z, t, rows, :] for t in range(nt)]
        up = x_up(k, False)
        for t in range(nt):
            fx[z, t, rows, :] = harmonic(k[t], up[t])

    def put_faces_y(z, start, size):
        for t in range(nt):
            fy[z, t, pl.ds(start, size), :] = harmonic(
                kb[z, t, pl.ds(start, size), :], kb[z, t, pl.ds(start + 1, size), :])

    def put_faces_z(z, start, size):
        for t in range(nt):
            fz[z, t, pl.ds(start, size), :] = harmonic(
                kb[z, t, pl.ds(start, size), :], kb[z + 1, t, pl.ds(start, size), :])

    def diagonal(base, z, start, size):
        rows = pl.ds(start, size)
        low_x = x_down([fx[z, t, rows, :] for t in range(nt)])
        out = []
        for t in range(nt):
            d = base[t] + fz[z - 1, t, rows, :] + fz[z, t, rows, :]
            d = d + fy[z, t, pl.ds(start - 1, size), :] + fy[z, t, rows, :]
            out.append(d + low_x[t] + fx[z, t, rows, :])
        return out

    def around(src, z, start, size):
        rows, under, over = pl.ds(start, size), pl.ds(start - 1, size), pl.ds(start + 1, size)
        mid_v = [src[z, t, rows, :] for t in range(nt)]
        face = [fx[z, t, rows, :] for t in range(nt)]
        up = x_up(mid_v, True)
        down = x_down([face[t] * mid_v[t] for t in range(nt)])
        out = []
        for t in range(nt):
            total = fz[z - 1, t, rows, :] * src[z - 1, t, rows, :] + fz[z, t, rows, :] * src[z + 1, t, rows, :]
            total = total + fy[z, t, under, :] * src[z, t, under, :] + fy[z, t, rows, :] * src[z, t, over, :]
            out.append(total + down[t] + face[t] * up[t])
        return out

    def begin(z, start, size):
        rows, inner = pl.ds(start, size), pl.ds(start - TOP, size)
        diag = diagonal([eb[z - HALO, t, inner, :] for t in range(nt)], z, start, size)
        near_sum = around(pb, z, start, size)
        for t in range(nt):
            d = diag[t]
            c = (1.0 - fb[z, t, rows, :].astype(F32)) / d
            db[z - HALO, t, inner, :] = d
            cb[z, t, rows, :] = c
            u0[z, t, rows, :] = c * (bb[z - HALO, t, inner, :] - (d * pb[z, t, rows, :] - near_sum[t]))

    def advance(src, dst, z, start, size):
        rows = pl.ds(start, size)
        new = around(src, z, start, size)
        for t in range(nt):
            dst[z, t, rows, :] = cb[z, t, rows, :] * new[t]

    @pl.loop(0, nz)
    def _(z):
        for t in range(nt):
            s, a, c, g, k = pick(zb[z + HALO, t, own, :], (stor, biot, coup, gain, perm))
            kb[z + HALO, t, own, :] = k
            gb[z, t] = g
            eb[z, t] = s + c
            bb[z, t] = s * ob[z, t] + c * pb[z + HALO, t, own, :] - a * sb[z, t] + qb[z, t]

    @pl.loop(HALO, far)
    def _(z):
        put_faces_y(z, TOP, ny - 1)
        put_faces_x(z, TOP, ny)

    @pl.loop(HALO, far - 1)
    def _(z):
        put_faces_z(z, TOP, ny)

    @pl.loop(HALO + 1, far - 1)
    def _(z):
        begin(z, TOP + 1, ny - 2)

    receive(first_z)

    def put_perm(z, start, size, live):
        row = lax.broadcasted_iota(jnp.int32, (size, LANES), 0) + start
        inside = ((row >= TOP) | has[-1][1]) & ((row < TOP + ny) | has[1][1]) & live
        for t in range(nt):
            (k,) = pick(zb[z, t, pl.ds(start, size), :], (perm,))
            kb[z, t, pl.ds(start, size), :] = jnp.where(inside, k, 0.0)

    put_perm(HALO - 1, TOP, ny, has[-1][0])
    put_perm(far, TOP, ny, has[1][0])
    put_faces_z(HALO - 1, TOP, ny)
    put_faces_z(far - 1, TOP, ny)

    begin(HALO, TOP + 1, ny - 2)
    begin(far - 1, TOP + 1, ny - 2)
    receive(first_y)

    for z in range(HALO, far):
        put_perm(z, TOP - 1, 1, has[0][0])
        put_perm(z, TOP + ny, 1, has[0][0])
        put_faces_y(z, TOP - 1, 1)
        put_faces_y(z, TOP + ny - 1, 1)
    for z in range(HALO, far):
        begin(z, TOP, 1)
        begin(z, TOP + ny - 1, 1)

    second_corners = [send(side, ((u0, two, two),)) for side in CORNERS]
    second = [send(side, ((u0, three, three),)) for side in FACES_Y + FACES_Z]

    @pl.loop(HALO + 1, far - 1)
    def _(z):
        advance(u0, u1, z, TOP + 1, ny - 2)

    @pl.loop(HALO + 2, far - 2)
    def _(z):
        advance(u1, u2, z, TOP + 2, ny - 4)

    receive(later)

    def put_scale(z, start, size):
        rows = pl.ds(start, size)
        base = [pick(zb[z, t, rows, :], (keep,))[0] for t in range(nt)]
        diag = diagonal(base, z, start, size)
        for t in range(nt):
            cb[z, t, rows, :] = (1.0 - fb[z, t, rows, :].astype(F32)) / diag[t]

    for z in range(HALO):
        put_perm(z, 5, 40, has[-1][0])
        put_perm(far + z, 5, 40, has[1][0])

    @pl.loop(HALO, far)
    def _(z):
        put_perm(z, 5, 3, has[0][0])
        put_perm(z, TOP + ny, 3, has[0][0])

    put_faces_z(0, 5, 40)
    for z in (1, 2, far, far + 1):
        put_faces_z(z, 5, 40)
        put_faces_y(z, 5, 38)
        put_faces_x(z, 5, 40)

    @pl.loop(HALO, far)
    def _(z):
        for start in (6, 40):
            put_faces_z(z, start, 2)
            put_faces_x(z, start, 2)
        put_faces_y(z, 5, 2)
        put_faces_y(z, 40, 2)

    for z in (1, 2, far, far + 1):
        put_scale(z, 6, 36)

    @pl.loop(HALO, far)
    def _(z):
        put_scale(z, 6, 2)
        put_scale(z, 40, 2)

    receive(second)
    receive(second_corners)

    for z in range(HALO + 1, far - 1):
        advance(u0, u1, z, 6, 3)
        advance(u0, u1, z, 39, 3)
    for z in (HALO, far - 1):
        advance(u0, u1, z, 6, 36)
    for z in (HALO - 1, far):
        advance(u0, u1, z, 7, 34)
    for z in (HALO - 2, far + 1):
        advance(u0, u1, z, 8, 32)

    advance(u1, u2, HALO - 1, TOP, ny)
    advance(u1, u2, far, TOP, ny)

    for z in (HALO, HALO + 1, far - 2, far - 1):
        advance(u1, u2, z, TOP - 1, ny + 2)

    for z in range(HALO + 2, far - 2):
        advance(u1, u2, z, TOP - 1, 3)
        advance(u1, u2, z, TOP + ny - 2, 3)

    def fold(v):
        total = v[0:8]
        for i in range(8, v.shape[0], 8):
            total = total + v[i:i + 8]
        return total

    def moment_step(z, acc):
        zz = z + HALO
        new = around(u2, zz, TOP, ny)
        acc = list(acc)
        for t in range(nt):
            d = db[z, t]
            last = (1.0 - fb[zz, t, own, :].astype(F32)) * new[t]
            w3[z, t] = last
            u = [u0[zz, t, own, :], u1[zz, t, own, :], u2[zz, t, own, :]]
            w = [d * v for v in u] + [last]
            for e, (i, j) in enumerate(((0, 0), (0, 1), (1, 1), (1, 2), (2, 2), (2, 3))):
                acc[e] = acc[e] + fold(u[i] * w[j])
        return tuple(acc)

    def norm_step(z, acc):
        zz = z + HALO
        acc = list(acc)
        for t in range(nt):
            d, g = db[z, t], gb[z, t]
            u = [u0[zz, t, own, :], u1[zz, t, own, :], u2[zz, t, own, :]]
            w = [d * v for v in u] + [w3[z, t]]
            s = [g * v for v in u]
            e = 0
            for i in range(4):
                for j in range(i, 4):
                    acc[e] = acc[e] + fold(w[i] * w[j])
                    e += 1
            for i in range(3):
                for j in range(i, 3):
                    acc[e] = acc[e] + fold(s[i] * s[j])
                    e += 1
        return tuple(acc)

    sub = lax.broadcasted_iota(jnp.int32, (8, LANES), 0)
    zero = jnp.zeros((8, LANES), F32)

    def merge(a, b, step):
        take = (sub & step) == 0
        return jnp.where(take, a, b) + pltpu.roll(jnp.where(take, b, a), step, 0)

    def in_lanes(acc):
        line = zero
        for i in range(0, len(acc), 8):
            eight = (acc[i:i + 8] + [zero] * 8)[:8]
            four = [merge(eight[j], eight[j + 1], 1) for j in range(0, 8, 2)]
            pair = [merge(four[j], four[j + 1], 2) for j in range(0, 4, 2)]
            whole = jnp.sum(merge(pair[0], pair[1], 4), axis=1, keepdims=True)
            line = line + jnp.where(lane == sub + i, whole, 0.0)
        return jnp.sum(line, axis=0, keepdims=True)

    def share(value, place, slots, rank, size, peer, out_sem, in_sem):
        lines[place] = value
        slots[rank] = value
        for j in range(1, size):
            pltpu.make_async_remote_copy(
                src_ref=lines.at[place], dst_ref=slots.at[rank], send_sem=out_sem, recv_sem=in_sem,
                device_id=peer(j), device_id_type=MESH).start()
        all_of = slots.at[pl.ds(0, size - 1)]
        return pltpu.make_async_remote_copy(
            src_ref=all_of, dst_ref=all_of, send_sem=out_sem, recv_sem=in_sem,
            device_id=peer(1), device_id_type=MESH)

    def gather(flight, slots, size):
        flight.wait_recv()
        total = [slots[j] for j in range(size)]
        while len(total) > 1:
            total = [total[j] + total[j + 1] for j in range(0, len(total), 2)]
        return total[0]

    acc = list(lax.fori_loop(0, nz // 2, lambda i, a: moment_step(2 * i + 1, moment_step(2 * i, a)), (zero,) * 6))
    flight_a1 = share(in_lanes(acc), 0, slots_a1, rank_a, size_a, peer_a, asem.at[0], arsem.at[0])
    acc = list(lax.fori_loop(0, nz, norm_step, (zero,) * 16))
    flight_a2 = share(in_lanes(acc), 1, slots_a2, rank_a, size_a, peer_a, asem.at[1], arsem.at[1])
    for side, copies in sent:
        @pl.when(exists(opposite(side)))
        def _():
            for copy in copies:
                copy.wait_send()
    part = gather(flight_a1, slots_a1, size_a)
    flight_b1 = share(part, 2, slots_b1, rank_b, size_b, peer_b, bsem.at[0], brsem.at[0])
    part = gather(flight_a2, slots_a2, size_a)
    flight_b2 = share(part, 3, slots_b2, rank_b, size_b, peer_b, bsem.at[1], brsem.at[1])
    flight_a1.wait_send()
    flight_a2.wait_send()
    total = gather(flight_b1, slots_b1, size_b)

    def at(e):
        return jnp.broadcast_to(total[:, e:e + 1], (1, LANES))

    m = [at(e) for e in range(6)]
    h = [m[i] - m[i + 1] for i in range(5)]
    l1, l2 = h[1] / h[0], h[2] / h[0]
    d1 = h[2] - l1 * h[1]
    e1 = h[3] - l1 * h[2]
    y1 = m[1] - l1 * m[0]
    ok1 = d1 > 1e-7 * h[2]
    safe1 = jnp.where(ok1, d1, 1.0)
    l3 = e1 / safe1
    d2 = h[4] - l2 * h[2] - l3 * e1
    y2 = m[2] - l2 * m[0] - l3 * y1
    ok2 = ok1 & (d2 > 1e-7 * h[4])
    c2 = jnp.where(ok2, y2 / jnp.where(ok2, d2, 1.0), 0.0)
    c1 = jnp.where(ok1, (y1 - e1 * c2) / safe1, 0.0)
    c0 = (m[0] - h[1] * c1 - h[2] * c2) / h[0]
    coef = [c0, c1, c2]

    b0, b1, b2 = [jnp.broadcast_to(v, (ny, LANES)) for v in coef]

    @pl.loop(0, nz)
    def _(z):
        zz = z + HALO
        for t in range(nt):
            delta = b0 * u0[zz, t, own, :] + b1 * u1[zz, t, own, :] + b2 * u2[zz, t, own, :]
            press_out[z, :, pl.ds(LANES * t, LANES)] = pb[zz, t, own, :] + delta
            strain_out[z, :, pl.ds(LANES * t, LANES)] = sb[z, t] + gb[z, t] * delta

    flight_b1.wait_send()
    flight_b2.wait_send()
    tail_out[0:1, :] = gather(flight_b2, slots_b2, size_b)
    for i in range(3):
        tail_out[i + 1:i + 2, :] = coef[i]


def norms(tail, cells):
    def at(e):
        return jnp.broadcast_to(tail[0:1, e:e + 1], (1, LANES))

    c = [tail[i:i + 1] for i in range(1, 4)]
    left = [1.0 - c[0], c[0] - c[1], c[1] - c[2], c[2]]
    e = 0
    out = []
    for v in (left, c):
        total = jnp.zeros((1, LANES), F32)
        for i in range(len(v)):
            for j in range(i, len(v)):
                total = total + (1.0 if i == j else 2.0) * v[i] * v[j] * at(e)
                e += 1
        out.append(total)
    lane = lax.broadcasted_iota(jnp.int32, (1, LANES), 1)
    return jnp.sqrt(jnp.maximum(jnp.where(lane == 0, out[0], out[1]), 0.0) / cells)


def solution(mesh):
    shape_z, shape_y = mesh.shape["gz"], mesh.shape["gy"]

    def per_device(zone_ids, fixed_cells, pressure_old, pressure_iter, strain_change, source,
                   zone_perm, zone_storage, zone_biot, zone_bulk):
        nz, ny, nx = zone_ids.shape
        nt = nx // LANES
        size_a = LINE * CORES
        size_b = shape_z * shape_y // size_a
        ext = (nz + 2 * HALO, nt, ny + 2 * TOP, LANES)
        inner = (nz, nt, ny, LANES)
        block = jax.ShapeDtypeStruct((nz, ny, nx), F32)
        dma = pltpu.SemaphoreType.DMA

        def kernel(*refs):
            body(shape_z, shape_y, nz, ny, nt, *refs)

        results = pl.pallas_call(
            kernel,
            out_shape=(pltpu.VMEM((nz, ny, nx), F32), pltpu.VMEM((nz, ny, nx), F32), pltpu.VMEM((8, LANES), F32)),
            in_specs=[pl.BlockSpec(memory_space=pl.ANY)] * 10,
            out_specs=tuple([pl.BlockSpec(memory_space=pltpu.VMEM)] * 3),
            scratch_shapes=[
                pltpu.VMEM(ext, jnp.int32), pltpu.VMEM(ext, jnp.int32),
            ] + [pltpu.VMEM(ext, F32)] * 9 + [pltpu.VMEM(inner, F32)] * 8 + [
                pltpu.SMEM((8,), F32), pltpu.SMEM((8,), F32), pltpu.SMEM((8,), F32), pltpu.SMEM((8,), F32),
                pltpu.VMEM((4, 1, LANES), F32),
                pltpu.VMEM((size_a, 1, LANES), F32), pltpu.VMEM((size_b, 1, LANES), F32),
                pltpu.VMEM((size_a, 1, LANES), F32), pltpu.VMEM((size_b, 1, LANES), F32),
                dma((4,)), dma((6,)), dma((32,)), dma((32,)),
                dma((2,)), dma((2,)), dma((2,)), dma((2,)),
            ],
            compiler_params=pltpu.CompilerParams(collective_id=0, has_side_effects=True),
        )(zone_ids, fixed_cells, pressure_old, pressure_iter, strain_change, source,
          zone_perm, zone_storage, zone_biot, zone_bulk)

        cells = float(nz * shape_z * ny * shape_y * nx)

        def emit(press_in, strain_in, tail_in, press_ref, strain_ref, norms_ref, sem):
            copies = []
            for i, (a, b) in enumerate(((press_in, press_ref), (strain_in, strain_ref))):
                for j in range(4):
                    part = pl.ds(j * nz // 4, nz // 4)
                    copy = pltpu.make_async_copy(a.at[part], b.at[part], sem.at[i, j])
                    copy.start()
                    copies.append(copy)
            both = norms(tail_in[...], cells)
            norms_ref[0] = both[0, 0]
            norms_ref[1] = both[0, 1]
            for copy in copies:
                copy.wait()

        return pl.pallas_call(
            emit,
            out_shape=(block, block, jax.ShapeDtypeStruct((2,), F32)),
            in_specs=[pl.BlockSpec(memory_space=pltpu.VMEM)] * 3,
            out_specs=(pl.BlockSpec(memory_space=pl.ANY),) * 2 + (pl.BlockSpec(memory_space=pltpu.SMEM),),
            scratch_shapes=[dma((2, 4))],
        )(*[pltpu.with_memory_space_constraint(v, pltpu.VMEM) for v in results])

    field = P("gz", "gy", None)
    return jax.shard_map(
        per_device, mesh=mesh,
        in_specs=(field,) * 6 + (P(),) * 4,
        out_specs=(field, field, P()),
        check_vma=False,
    )
```

```python
import jax
import jax.numpy as jnp
from jax import lax
from jax.experimental import pallas as pl
from jax.experimental.pallas import tpu as pltpu
from jax.sharding import PartitionSpec as P

MESH = pl.DeviceIdType.MESH
F32 = jnp.float32
CORES = 2
LINE = 8
LANES = 128
HALO = 3
TOP = 8


def halo_box(side, layers_z, layers_y, nz, ny):
    def one(toward, layers, base, size):
        low, high = layers
        if toward == 0:
            return base, base, size
        if toward > 0:
            return base + low, base + size + low, high - low
        return base + size - high, base - high, high - low

    sz, dz, lz = one(side[0], layers_z, HALO, nz)
    sy, dy, ly = one(side[1], layers_y, TOP, ny)
    src = (pl.ds(sz, lz), slice(None), pl.ds(sy, ly))
    dst = (pl.ds(dz, lz), slice(None), pl.ds(dy, ly))
    return src, dst


FACES_Z = ((-1, 0), (1, 0))
FACES_Y = ((0, -1), (0, 1))
CORNERS = ((-1, -1), (-1, 1), (1, -1), (1, 1))
ALL = FACES_Z + FACES_Y + CORNERS


def pick(zone, table):
    b0 = (zone & 1) != 0
    b1 = (zone & 2) != 0
    b2 = (zone & 4) != 0

    def one(t):
        low = [jnp.where(b0, t[2 * i + 1], t[2 * i]) for i in range(4)]
        mid = [jnp.where(b1, low[2 * i + 1], low[2 * i]) for i in range(2)]
        return jnp.where(b2, mid[1], mid[0])

    return [one(t) for t in table]


def harmonic(a, b):
    return 2.0 * a * b / jnp.maximum(a + b, 1e-20)


def body(shape_z, shape_y, nz, ny, nt, zone_hbm, fixed_hbm, old_hbm, iter_hbm, strain_hbm,
         source_hbm, perm_hbm, stor_hbm, biot_hbm, bulk_hbm, press_out, strain_out, tail_out,
         zb, fb, pb, kb, fx, fy, fz, cb, u0, u1, u2, db, gb, bb, ob, sb, qb, eb, w3,
         perm_s, stor_s, biot_s, bulk_s, lines, slots_a1, slots_b1, slots_a2, slots_b2,
         tsem, lsem, ssem, rsem, asem, arsem, bsem, brsem):
    gz = lax.axis_index("gz")
    gy = lax.axis_index("gy")
    chips = shape_z // CORES
    rows_y = shape_y // LINE
    my_x, my_core = gz // CORES, gz % CORES
    my_y, my_z = gy // LINE, gy % LINE
    has = {-1: (gz > 0, gy > 0), 0: (gz >= 0, gy >= 0), 1: (gz < shape_z - 1, gy < shape_y - 1)}

    def exists(side):
        return has[side[0]][0] & has[side[1]][1]

    def opposite(side):
        return (-side[0], -side[1])

    size_a = LINE * CORES
    size_b = chips * rows_y
    rank_a = my_z * CORES + my_core
    rank_b = my_y * chips + my_x

    def wrap(value, size):
        return jnp.where(value >= size, value - size, value)

    def peer_a(j):
        return (my_x * CORES + wrap(my_core + j % CORES, CORES), my_y * LINE + wrap(my_z + j // CORES, LINE))

    def peer_b(j):
        return (wrap(my_x + j % chips, chips) * CORES + my_core, wrap(my_y + j // chips, rows_y) * LINE + my_z)

    barrier = pltpu.get_barrier_semaphore()
    for j in range(1, size_a):
        pl.semaphore_signal(barrier, inc=1, device_id=peer_a(j), device_id_type=MESH)
    for j in range(1, size_b):
        pl.semaphore_signal(barrier, inc=1, device_id=peer_b(j), device_id_type=MESH)
    expected = size_a - 1 + size_b - 1
    for side in CORNERS + FACES_Y + FACES_Z:
        expected = expected + jnp.where(exists(side), 1, 0)

        @pl.when(exists(side))
        def _():
            pl.semaphore_signal(barrier, inc=1, device_id=(gz + side[0], gy + side[1]), device_id_type=MESH)

    loads = []
    for n, (src, dst, ext) in enumerate((
        (zone_hbm, zb, True), (iter_hbm, pb, True), (fixed_hbm, fb, True),
        (old_hbm, ob, False), (strain_hbm, sb, False), (source_hbm, qb, False),
    )):
        for t in range(nt):
            view = src.at[:, :, pl.ds(LANES * t, LANES)]
            if ext:
                into = dst.at[pl.ds(HALO, nz), t, pl.ds(TOP, ny), :]
            else:
                into = dst.at[:, t]
            pltpu.make_async_copy(view, into, lsem.at[n]).start()
        whole = dst.at[pl.ds(HALO, nz), :, pl.ds(TOP, ny), :] if ext else dst
        loads.append([pltpu.make_async_copy(whole, whole, lsem.at[n])])

    tables = []
    for i, (src, dst) in enumerate(((perm_hbm, perm_s), (stor_hbm, stor_s), (biot_hbm, biot_s), (bulk_hbm, bulk_s))):
        copy = pltpu.make_async_copy(src, dst, tsem.at[i])
        copy.start()
        tables.append(copy)

    own = pl.ds(TOP, ny)
    far = HALO + nz

    def clear_planes(z0):
        for t in range(nt):
            for z in range(z0, z0 + HALO):
                u0[z, t] = jnp.zeros(u0.shape[2:], F32)
                pb[z, t] = jnp.zeros(pb.shape[2:], F32)

    def clear_rows(start):
        @pl.loop(0, nz + 2 * HALO)
        def _(z):
            for t in range(nt):
                u0[z, t, pl.ds(start, TOP), :] = jnp.zeros((TOP, LANES), F32)
                pb[z, t, pl.ds(start, TOP), :] = jnp.zeros((TOP, LANES), F32)

    @pl.when(gz == 0)
    def _():
        clear_planes(0)

    @pl.when(gz == shape_z - 1)
    def _():
        clear_planes(far)

    @pl.when(gy == 0)
    def _():
        clear_rows(0)

    @pl.when(gy == shape_y - 1)
    def _():
        clear_rows(TOP + ny)

    for group in loads[:2]:
        for copy in group:
            copy.wait()
    pl.semaphore_wait(barrier, expected)

    counter = [0]
    sent = {}

    def send(side, parts):
        i = counter[0]
        counter[0] += 1
        sems = dict(send_sem=ssem.at[ALL.index(side)], recv_sem=rsem.at[i],
                    device_id=(gz - side[0], gy - side[1]), device_id_type=MESH)
        copies, units = [], 0
        for ref, layers_z, layers_y in parts:
            src, dst = halo_box(side, layers_z, layers_y, nz, ny)
            copies.append(pltpu.make_async_remote_copy(src_ref=ref.at[src], dst_ref=ref.at[dst], **sems))
            wide, tall = layers_z[1] - layers_z[0], layers_y[1] - layers_y[0]
            units += (wide if side[0] else 1) * (tall if side[1] else 1)

        @pl.when(exists(opposite(side)))
        def _():
            for copy in copies:
                copy.start()
        sent[side] = sent.get(side, 0) + units
        return side, units, sems

    def bytes_of(side, units, sems):
        if side[1] == 0:
            box = pb.at[pl.ds(0, units), :, own, :]
        elif side[0] == 0:
            box = pb.at[pl.ds(HALO, nz), :, pl.ds(0, units), :]
        else:
            box = pb.at[pl.ds(0, units), :, pl.ds(0, 1), :]
        return pltpu.make_async_remote_copy(src_ref=box, dst_ref=box, **sems)

    def receive(group):
        for side, units, sems in group:
            @pl.when(exists(side))
            def _():
                bytes_of(side, units, sems).wait_recv()

    one, rest, two, three = (0, 1), (1, 3), (0, 2), (0, 3)
    first_y = [send(side, ((pb, one, one), (zb, one, one))) for side in FACES_Y]
    first_z = [send(side, ((pb, one, one), (zb, one, one))) for side in FACES_Z]
    for copy in loads[2]:
        copy.wait()
    later = [send(side, ((zb, two, two), (fb, one, one))) for side in CORNERS]
    later += [send(side, ((zb, rest, rest), (fb, two, two))) for side in FACES_Y + FACES_Z]

    for group in loads[3:]:
        for copy in group:
            copy.wait()

    for copy in tables:
        copy.wait()
    perm = [perm_s[i] for i in range(8)]
    stor = [stor_s[i] for i in range(8)]
    biot = [biot_s[i] for i in range(8)]
    gain = [biot_s[i] / bulk_s[i] for i in range(8)]
    coup = [biot[i] * biot[i] / bulk_s[i] for i in range(8)]
    keep = [stor[i] + coup[i] for i in range(8)]

    lane = lax.broadcasted_iota(jnp.int32, (8, LANES), 1)

    def x_up(tiles, wrap):
        rolled = [pltpu.roll(v, LANES - 1, 1) for v in tiles]
        last = lax.broadcasted_iota(jnp.int32, tiles[0].shape, 1) == LANES - 1
        out = []
        for t in range(nt):
            nxt = rolled[t + 1] if t + 1 < nt else (rolled[0] if wrap else jnp.zeros_like(rolled[0]))
            out.append(jnp.where(last, nxt, rolled[t]))
        return out

    def x_down(tiles):
        rolled = [pltpu.roll(v, 1, 1) for v in tiles]
        head = lax.broadcasted_iota(jnp.int32, tiles[0].shape, 1) == 0
        return [jnp.where(head, rolled[t - 1], rolled[t]) for t in range(nt)]

    def put_faces_x(z, start, size):
        rows = pl.ds(start, size)
        k = [kb[z, t, rows, :] for t in range(nt)]
        up = x_up(k, False)
        for t in range(nt):
            fx[z, t, rows, :] = harmonic(k[t], up[t])

    def put_faces_y(z, start, size):
        for t in range(nt):
            fy[z, t, pl.ds(start, size), :] = harmonic(
                kb[z, t, pl.ds(start, size), :], kb[z, t, pl.ds(start + 1, size), :])

    def put_faces_z(z, start, size):
        for t in range(nt):
            fz[z, t, pl.ds(start, size), :] = harmonic(
                kb[z, t, pl.ds(start, size), :], kb[z + 1, t, pl.ds(start, size), :])

    def diagonal(base, z, start, size):
        rows = pl.ds(start, size)
        low_x = x_down([fx[z, t, rows, :] for t in range(nt)])
        out = []
        for t in range(nt):
            d = base[t] + fz[z - 1, t, rows, :] + fz[z, t, rows, :]
            d = d + fy[z, t, pl.ds(start - 1, size), :] + fy[z, t, rows, :]
            out.append(d + low_x[t] + fx[z, t, rows, :])
        return out

    def around(src, z, start, size):
        rows, under, over = pl.ds(start, size), pl.ds(start - 1, size), pl.ds(start + 1, size)
        mid_v = [src[z, t, rows, :] for t in range(nt)]
        face = [fx[z, t, rows, :] for t in range(nt)]
        up = x_up(mid_v, True)
        down = x_down([face[t] * mid_v[t] for t in range(nt)])
        out = []
        for t in range(nt):
            total = fz[z - 1, t, rows, :] * src[z - 1, t, rows, :] + fz[z, t, rows, :] * src[z + 1, t, rows, :]
            total = total + fy[z, t, under, :] * src[z, t, under, :] + fy[z, t, rows, :] * src[z, t, over, :]
            out.append(total + down[t] + face[t] * up[t])
        return out

    def begin(z, start, size):
        rows, inner = pl.ds(start, size), pl.ds(start - TOP, size)
        diag = diagonal([eb[z - HALO, t, inner, :] for t in range(nt)], z, start, size)
        near_sum = around(pb, z, start, size)
        for t in range(nt):
            d = diag[t]
            c = (1.0 - fb[z, t, rows, :].astype(F32)) / d
            db[z - HALO, t, inner, :] = d
            cb[z, t, rows, :] = c
            u0[z, t, rows, :] = c * (bb[z - HALO, t, inner, :] - (d * pb[z, t, rows, :] - near_sum[t]))

    def advance(src, dst, z, start, size):
        rows = pl.ds(start, size)
        new = around(src, z, start, size)
        for t in range(nt):
            dst[z, t, rows, :] = cb[z, t, rows, :] * new[t]

    @pl.loop(0, nz)
    def _(z):
        for t in range(nt):
            s, a, c, g, k = pick(zb[z + HALO, t, own, :], (stor, biot, coup, gain, perm))
            kb[z + HALO, t, own, :] = k
            gb[z, t] = g
            eb[z, t] = s + c
            bb[z, t] = s * ob[z, t] + c * pb[z + HALO, t, own, :] - a * sb[z, t] + qb[z, t]

    @pl.loop(HALO, far)
    def _(z):
        put_faces_y(z, TOP, ny - 1)
        put_faces_x(z, TOP, ny)

    @pl.loop(HALO, far - 1)
    def _(z):
        put_faces_z(z, TOP, ny)

    @pl.loop(HALO + 1, far - 1)
    def _(z):
        begin(z, TOP + 1, ny - 2)

    receive(first_z)

    def put_perm(z, start, size, live):
        row = lax.broadcasted_iota(jnp.int32, (size, LANES), 0) + start
        inside = ((row >= TOP) | has[-1][1]) & ((row < TOP + ny) | has[1][1]) & live
        for t in range(nt):
            (k,) = pick(zb[z, t, pl.ds(start, size), :], (perm,))
            kb[z, t, pl.ds(start, size), :] = jnp.where(inside, k, 0.0)

    put_perm(HALO - 1, TOP, ny, has[-1][0])
    put_perm(far, TOP, ny, has[1][0])
    put_faces_z(HALO - 1, TOP, ny)
    put_faces_z(far - 1, TOP, ny)

    begin(HALO, TOP + 1, ny - 2)
    begin(far - 1, TOP + 1, ny - 2)
    receive(first_y)

    for z in range(HALO, far):
        put_perm(z, TOP - 1, 1, has[0][0])
        put_perm(z, TOP + ny, 1, has[0][0])
        put_faces_y(z, TOP - 1, 1)
        put_faces_y(z, TOP + ny - 1, 1)
    for z in range(HALO, far):
        begin(z, TOP, 1)
        begin(z, TOP + ny - 1, 1)

    second_corners = [send(side, ((u0, two, two),)) for side in CORNERS]
    second = [send(side, ((u0, three, three),)) for side in FACES_Y + FACES_Z]

    @pl.loop(HALO + 1, far - 1)
    def _(z):
        advance(u0, u1, z, TOP + 1, ny - 2)

    @pl.loop(HALO + 2, far - 2)
    def _(z):
        advance(u1, u2, z, TOP + 2, ny - 4)

    receive(later)

    def put_scale(z, start, size):
        rows = pl.ds(start, size)
        base = [pick(zb[z, t, rows, :], (keep,))[0] for t in range(nt)]
        diag = diagonal(base, z, start, size)
        for t in range(nt):
            cb[z, t, rows, :] = (1.0 - fb[z, t, rows, :].astype(F32)) / diag[t]

    for z in range(HALO):
        put_perm(z, 5, 40, has[-1][0])
        put_perm(far + z, 5, 40, has[1][0])

    @pl.loop(HALO, far)
    def _(z):
        put_perm(z, 5, 3, has[0][0])
        put_perm(z, TOP + ny, 3, has[0][0])

    put_faces_z(0, 5, 40)
    for z in (1, 2, far, far + 1):
        put_faces_z(z, 5, 40)
        put_faces_y(z, 5, 38)
        put_faces_x(z, 5, 40)

    @pl.loop(HALO, far)
    def _(z):
        for start in (6, 40):
            put_faces_z(z, start, 2)
            put_faces_x(z, start, 2)
        put_faces_y(z, 5, 2)
        put_faces_y(z, 40, 2)

    for z in (1, 2, far, far + 1):
        put_scale(z, 6, 36)

    @pl.loop(HALO, far)
    def _(z):
        put_scale(z, 6, 2)
        put_scale(z, 40, 2)

    receive(second)
    receive(second_corners)

    for z in range(HALO + 1, far - 1):
        advance(u0, u1, z, 6, 3)
        advance(u0, u1, z, 39, 3)
    for z in (HALO, far - 1):
        advance(u0, u1, z, 6, 36)
    for z in (HALO - 1, far):
        advance(u0, u1, z, 7, 34)
    for z in (HALO - 2, far + 1):
        advance(u0, u1, z, 8, 32)

    advance(u1, u2, HALO - 1, TOP, ny)
    advance(u1, u2, far, TOP, ny)

    for z in (HALO, HALO + 1, far - 2, far - 1):
        advance(u1, u2, z, TOP - 1, ny + 2)

    for z in range(HALO + 2, far - 2):
        advance(u1, u2, z, TOP - 1, 3)
        advance(u1, u2, z, TOP + ny - 2, 3)

    def fold(v):
        total = v[0:8]
        for i in range(8, v.shape[0], 8):
            total = total + v[i:i + 8]
        return total

    def moment_step(z, acc):
        zz = z + HALO
        new = around(u2, zz, TOP, ny)
        acc = list(acc)
        for t in range(nt):
            d = db[z, t]
            last = (1.0 - fb[zz, t, own, :].astype(F32)) * new[t]
            w3[z, t] = last
            u = [u0[zz, t, own, :], u1[zz, t, own, :], u2[zz, t, own, :]]
            w = [d * v for v in u] + [last]
            for e, (i, j) in enumerate(((0, 0), (0, 1), (1, 1), (1, 2), (2, 2), (2, 3))):
                acc[e] = acc[e] + fold(u[i] * w[j])
        return tuple(acc)

    def norm_step(z, acc):
        zz = z + HALO
        acc = list(acc)
        for t in range(nt):
            d, g = db[z, t], gb[z, t]
            u = [u0[zz, t, own, :], u1[zz, t, own, :], u2[zz, t, own, :]]
            w = [d * v for v in u] + [w3[z, t]]
            s = [g * v for v in u]
            e = 0
            for i in range(4):
                for j in range(i, 4):
                    acc[e] = acc[e] + fold(w[i] * w[j])
                    e += 1
            for i in range(3):
                for j in range(i, 3):
                    acc[e] = acc[e] + fold(s[i] * s[j])
                    e += 1
        return tuple(acc)

    sub = lax.broadcasted_iota(jnp.int32, (8, LANES), 0)
    zero = jnp.zeros((8, LANES), F32)

    def merge(a, b, step):
        take = (sub & step) == 0
        return jnp.where(take, a, b) + pltpu.roll(jnp.where(take, b, a), step, 0)

    def in_lanes(acc):
        line = zero
        for i in range(0, len(acc), 8):
            eight = (acc[i:i + 8] + [zero] * 8)[:8]
            four = [merge(eight[j], eight[j + 1], 1) for j in range(0, 8, 2)]
            pair = [merge(four[j], four[j + 1], 2) for j in range(0, 4, 2)]
            whole = jnp.sum(merge(pair[0], pair[1], 4), axis=1, keepdims=True)
            line = line + jnp.where(lane == sub + i, whole, 0.0)
        return jnp.sum(line, axis=0, keepdims=True)

    def share(value, place, slots, rank, size, peer, out_sem, in_sem):
        lines[place] = value
        slots[rank] = value
        for j in range(1, size):
            pltpu.make_async_remote_copy(
                src_ref=lines.at[place], dst_ref=slots.at[rank], send_sem=out_sem, recv_sem=in_sem,
                device_id=peer(j), device_id_type=MESH).start()
        all_of = slots.at[pl.ds(0, size - 1)]
        return pltpu.make_async_remote_copy(
            src_ref=all_of, dst_ref=all_of, send_sem=out_sem, recv_sem=in_sem,
            device_id=peer(1), device_id_type=MESH)

    def gather(flight, slots, size):
        flight.wait_recv()
        total = [slots[j] for j in range(size)]
        while len(total) > 1:
            total = [total[j] + total[j + 1] for j in range(0, len(total), 2)]
        return total[0]

    acc = list(lax.fori_loop(0, nz // 2, lambda i, a: moment_step(2 * i + 1, moment_step(2 * i, a)), (zero,) * 6))
    flight_a1 = share(in_lanes(acc), 0, slots_a1, rank_a, size_a, peer_a, asem.at[0], arsem.at[0])
    acc = list(lax.fori_loop(0, nz, norm_step, (zero,) * 16))
    flight_a2 = share(in_lanes(acc), 1, slots_a2, rank_a, size_a, peer_a, asem.at[1], arsem.at[1])
    for side, units, sems in second + second_corners:
        @pl.when(exists(opposite(side)))
        def _():
            bytes_of(side, sent[side], sems).wait_send()
    part = gather(flight_a1, slots_a1, size_a)
    flight_b1 = share(part, 2, slots_b1, rank_b, size_b, peer_b, bsem.at[0], brsem.at[0])
    part = gather(flight_a2, slots_a2, size_a)
    flight_b2 = share(part, 3, slots_b2, rank_b, size_b, peer_b, bsem.at[1], brsem.at[1])
    flight_a1.wait_send()
    flight_a2.wait_send()
    total = gather(flight_b1, slots_b1, size_b)

    def at(e):
        return jnp.broadcast_to(total[:, e:e + 1], (1, LANES))

    m = [at(e) for e in range(6)]
    h = [m[i] - m[i + 1] for i in range(5)]
    l1, l2 = h[1] / h[0], h[2] / h[0]
    d1 = h[2] - l1 * h[1]
    e1 = h[3] - l1 * h[2]
    y1 = m[1] - l1 * m[0]
    ok1 = d1 > 1e-7 * h[2]
    safe1 = jnp.where(ok1, d1, 1.0)
    l3 = e1 / safe1
    d2 = h[4] - l2 * h[2] - l3 * e1
    y2 = m[2] - l2 * m[0] - l3 * y1
    ok2 = ok1 & (d2 > 1e-7 * h[4])
    c2 = jnp.where(ok2, y2 / jnp.where(ok2, d2, 1.0), 0.0)
    c1 = jnp.where(ok1, (y1 - e1 * c2) / safe1, 0.0)
    c0 = (m[0] - h[1] * c1 - h[2] * c2) / h[0]
    coef = [c0, c1, c2]

    b0, b1, b2 = [jnp.broadcast_to(v, (ny, LANES)) for v in coef]

    @pl.loop(0, nz)
    def _(z):
        zz = z + HALO
        for t in range(nt):
            delta = b0 * u0[zz, t, own, :] + b1 * u1[zz, t, own, :] + b2 * u2[zz, t, own, :]
            press_out[z, :, pl.ds(LANES * t, LANES)] = pb[zz, t, own, :] + delta
            strain_out[z, :, pl.ds(LANES * t, LANES)] = sb[z, t] + gb[z, t] * delta

    flight_b1.wait_send()
    flight_b2.wait_send()
    tail_out[0:1, :] = gather(flight_b2, slots_b2, size_b)
    for i in range(3):
        tail_out[i + 1:i + 2, :] = coef[i]


def norms(tail, cells):
    def at(e):
        return jnp.broadcast_to(tail[0:1, e:e + 1], (1, LANES))

    c = [tail[i:i + 1] for i in range(1, 4)]
    left = [1.0 - c[0], c[0] - c[1], c[1] - c[2], c[2]]
    e = 0
    out = []
    for v in (left, c):
        total = jnp.zeros((1, LANES), F32)
        for i in range(len(v)):
            for j in range(i, len(v)):
                total = total + (1.0 if i == j else 2.0) * v[i] * v[j] * at(e)
                e += 1
        out.append(total)
    lane = lax.broadcasted_iota(jnp.int32, (1, LANES), 1)
    return jnp.sqrt(jnp.maximum(jnp.where(lane == 0, out[0], out[1]), 0.0) / cells)


def solution(mesh):
    shape_z, shape_y = mesh.shape["gz"], mesh.shape["gy"]

    def per_device(zone_ids, fixed_cells, pressure_old, pressure_iter, strain_change, source,
                   zone_perm, zone_storage, zone_biot, zone_bulk):
        nz, ny, nx = zone_ids.shape
        nt = nx // LANES
        size_a = LINE * CORES
        size_b = shape_z * shape_y // size_a
        ext = (nz + 2 * HALO, nt, ny + 2 * TOP, LANES)
        inner = (nz, nt, ny, LANES)
        block = jax.ShapeDtypeStruct((nz, ny, nx), F32)
        dma = pltpu.SemaphoreType.DMA

        def kernel(*refs):
            body(shape_z, shape_y, nz, ny, nt, *refs)

        results = pl.pallas_call(
            kernel,
            out_shape=(pltpu.VMEM((nz, ny, nx), F32), pltpu.VMEM((nz, ny, nx), F32), pltpu.VMEM((8, LANES), F32)),
            in_specs=[pl.BlockSpec(memory_space=pl.ANY)] * 10,
            out_specs=tuple([pl.BlockSpec(memory_space=pltpu.VMEM)] * 3),
            scratch_shapes=[
                pltpu.VMEM(ext, jnp.int32), pltpu.VMEM(ext, jnp.int32),
            ] + [pltpu.VMEM(ext, F32)] * 9 + [pltpu.VMEM(inner, F32)] * 8 + [
                pltpu.SMEM((8,), F32), pltpu.SMEM((8,), F32), pltpu.SMEM((8,), F32), pltpu.SMEM((8,), F32),
                pltpu.VMEM((4, 1, LANES), F32),
                pltpu.VMEM((size_a, 1, LANES), F32), pltpu.VMEM((size_b, 1, LANES), F32),
                pltpu.VMEM((size_a, 1, LANES), F32), pltpu.VMEM((size_b, 1, LANES), F32),
                dma((4,)), dma((6,)), dma((8,)), dma((20,)),
                dma((2,)), dma((2,)), dma((2,)), dma((2,)),
            ],
            compiler_params=pltpu.CompilerParams(collective_id=0, has_side_effects=True),
        )(zone_ids, fixed_cells, pressure_old, pressure_iter, strain_change, source,
          zone_perm, zone_storage, zone_biot, zone_bulk)

        cells = float(nz * shape_z * ny * shape_y * nx)

        def emit(press_in, strain_in, tail_in, press_ref, strain_ref, norms_ref, pair, sem, pair_sem):
            copies = []
            for i, (a, b) in enumerate(((press_in, press_ref), (strain_in, strain_ref))):
                for j in range(4):
                    part = pl.ds(j * nz // 4, nz // 4)
                    copy = pltpu.make_async_copy(a.at[part], b.at[part], sem.at[i, j])
                    copy.start()
                    copies.append(copy)
            both = norms(tail_in[...], cells)
            pair[0] = both[0, 0]
            pair[1] = both[0, 1]
            copy = pltpu.make_async_copy(pair, norms_ref, pair_sem)
            copy.start()
            copies.append(copy)
            for copy in copies:
                copy.wait()

        return pl.pallas_call(
            emit,
            out_shape=(block, block, jax.ShapeDtypeStruct((2,), F32)),
            in_specs=[pl.BlockSpec(memory_space=pltpu.VMEM)] * 3,
            out_specs=(pl.BlockSpec(memory_space=pl.ANY),) * 3,
            scratch_shapes=[pltpu.SMEM((2,), F32), dma((2, 4)), dma],
        )(*[pltpu.with_memory_space_constraint(v, pltpu.VMEM) for v in results])

    field = P("gz", "gy", None)
    return jax.shard_map(
        per_device, mesh=mesh,
        in_specs=(field,) * 6 + (P(),) * 4,
        out_specs=(field, field, P()),
        check_vma=False,
    )
```

```python
import jax
import jax.numpy as jnp
from jax import lax
from jax.experimental import pallas as pl
from jax.experimental.pallas import tpu as pltpu
from jax.sharding import PartitionSpec as P

MESH = pl.DeviceIdType.MESH
F32 = jnp.float32
CORES = 2
LINE = 8
LANES = 128
HALO = 3
TOP = 8


def halo_box(side, layers_z, layers_y, nz, ny):
    def one(toward, layers, base, size):
        low, high = layers
        if toward == 0:
            return base, base, size
        if toward > 0:
            return base + low, base + size + low, high - low
        return base + size - high, base - high, high - low

    sz, dz, lz = one(side[0], layers_z, HALO, nz)
    sy, dy, ly = one(side[1], layers_y, TOP, ny)
    src = (pl.ds(sz, lz), slice(None), pl.ds(sy, ly))
    dst = (pl.ds(dz, lz), slice(None), pl.ds(dy, ly))
    return src, dst


FACES_Z = ((-1, 0), (1, 0))
FACES_Y = ((0, -1), (0, 1))
CORNERS = ((-1, -1), (-1, 1), (1, -1), (1, 1))
ALL = FACES_Z + FACES_Y + CORNERS


def pick(zone, table):
    b0 = (zone & 1) != 0
    b1 = (zone & 2) != 0
    b2 = (zone & 4) != 0

    def one(t):
        low = [jnp.where(b0, t[2 * i + 1], t[2 * i]) for i in range(4)]
        mid = [jnp.where(b1, low[2 * i + 1], low[2 * i]) for i in range(2)]
        return jnp.where(b2, mid[1], mid[0])

    return [one(t) for t in table]


def harmonic(a, b):
    return 2.0 * a * b / jnp.maximum(a + b, 1e-20)


def body(shape_z, shape_y, nz, ny, nt, zone_hbm, fixed_hbm, old_hbm, iter_hbm, strain_hbm,
         source_hbm, perm_hbm, stor_hbm, biot_hbm, bulk_hbm, press_out, strain_out, tail_out,
         zb, fb, pb, kb, fx, fy, fz, cb, u0, u1, u2, db, gb, bb, ob, sb, qb, eb, w3,
         perm_s, stor_s, biot_s, bulk_s, lines, slots_a1, slots_b1, slots_a2, slots_b2,
         tsem, lsem, ssem, rsem, asem, arsem, bsem, brsem):
    gz = lax.axis_index("gz")
    gy = lax.axis_index("gy")
    chips = shape_z // CORES
    rows_y = shape_y // LINE
    my_x, my_core = gz // CORES, gz % CORES
    my_y, my_z = gy // LINE, gy % LINE
    has = {-1: (gz > 0, gy > 0), 0: (gz >= 0, gy >= 0), 1: (gz < shape_z - 1, gy < shape_y - 1)}

    def exists(side):
        return has[side[0]][0] & has[side[1]][1]

    def opposite(side):
        return (-side[0], -side[1])

    size_a = LINE * CORES
    size_b = chips * rows_y
    rank_a = my_z * CORES + my_core
    rank_b = my_y * chips + my_x

    def wrap(value, size):
        return jnp.where(value >= size, value - size, value)

    def peer_a(j):
        return (my_x * CORES + wrap(my_core + j % CORES, CORES), my_y * LINE + wrap(my_z + j // CORES, LINE))

    def peer_b(j):
        return (wrap(my_x + j % chips, chips) * CORES + my_core, wrap(my_y + j // chips, rows_y) * LINE + my_z)

    barrier = pltpu.get_barrier_semaphore()
    for j in range(1, size_a):
        pl.semaphore_signal(barrier, inc=1, device_id=peer_a(j), device_id_type=MESH)
    for j in range(1, size_b):
        pl.semaphore_signal(barrier, inc=1, device_id=peer_b(j), device_id_type=MESH)
    expected = size_a - 1 + size_b - 1
    for side in CORNERS + FACES_Y + FACES_Z:
        expected = expected + jnp.where(exists(side), 1, 0)

        @pl.when(exists(side))
        def _():
            pl.semaphore_signal(barrier, inc=1, device_id=(gz + side[0], gy + side[1]), device_id_type=MESH)

    loads = []
    for n, (src, dst, ext) in enumerate((
        (zone_hbm, zb, True), (iter_hbm, pb, True), (fixed_hbm, fb, True),
        (old_hbm, ob, False), (strain_hbm, sb, False), (source_hbm, qb, False),
    )):
        for t in range(nt):
            view = src.at[:, :, pl.ds(LANES * t, LANES)]
            if ext:
                into = dst.at[pl.ds(HALO, nz), t, pl.ds(TOP, ny), :]
            else:
                into = dst.at[:, t]
            pltpu.make_async_copy(view, into, lsem.at[n]).start()
        whole = dst.at[pl.ds(HALO, nz), :, pl.ds(TOP, ny), :] if ext else dst
        loads.append([pltpu.make_async_copy(whole, whole, lsem.at[n])])

    tables = []
    for i, (src, dst) in enumerate(((perm_hbm, perm_s), (stor_hbm, stor_s), (biot_hbm, biot_s), (bulk_hbm, bulk_s))):
        copy = pltpu.make_async_copy(src, dst, tsem.at[i])
        copy.start()
        tables.append(copy)

    own = pl.ds(TOP, ny)
    far = HALO + nz

    def clear_planes(z0):
        for t in range(nt):
            for z in range(z0, z0 + HALO):
                u0[z, t] = jnp.zeros(u0.shape[2:], F32)
                pb[z, t] = jnp.zeros(pb.shape[2:], F32)

    def clear_rows(start):
        @pl.loop(0, nz + 2 * HALO)
        def _(z):
            for t in range(nt):
                u0[z, t, pl.ds(start, TOP), :] = jnp.zeros((TOP, LANES), F32)
                pb[z, t, pl.ds(start, TOP), :] = jnp.zeros((TOP, LANES), F32)

    @pl.when(gz == 0)
    def _():
        clear_planes(0)

    @pl.when(gz == shape_z - 1)
    def _():
        clear_planes(far)

    @pl.when(gy == 0)
    def _():
        clear_rows(0)

    @pl.when(gy == shape_y - 1)
    def _():
        clear_rows(TOP + ny)

    for group in loads[:2]:
        for copy in group:
            copy.wait()
    pl.semaphore_wait(barrier, expected)

    counter = [0]
    sent = {}

    def send(side, parts):
        i = counter[0]
        counter[0] += 1
        sems = dict(send_sem=ssem.at[ALL.index(side)], recv_sem=rsem.at[i],
                    device_id=(gz - side[0], gy - side[1]), device_id_type=MESH)
        copies, units = [], 0
        for ref, layers_z, layers_y in parts:
            src, dst = halo_box(side, layers_z, layers_y, nz, ny)
            copies.append(pltpu.make_async_remote_copy(src_ref=ref.at[src], dst_ref=ref.at[dst], **sems))
            wide, tall = layers_z[1] - layers_z[0], layers_y[1] - layers_y[0]
            units += (wide if side[0] else 1) * (tall if side[1] else 1)

        @pl.when(exists(opposite(side)))
        def _():
            for copy in copies:
                copy.start()
        sent[side] = sent.get(side, 0) + units
        return side, units, sems

    def bytes_of(side, units, sems):
        if side[1] == 0:
            box = pb.at[pl.ds(0, units), :, own, :]
        elif side[0] == 0:
            box = pb.at[pl.ds(HALO, nz), :, pl.ds(0, units), :]
        else:
            box = pb.at[pl.ds(0, units), :, pl.ds(0, 1), :]
        return pltpu.make_async_remote_copy(src_ref=box, dst_ref=box, **sems)

    def receive(group):
        for side, units, sems in group:
            @pl.when(exists(side))
            def _():
                bytes_of(side, units, sems).wait_recv()

    one, rest, two, three = (0, 1), (1, 3), (0, 2), (0, 3)
    first_y = [send(side, ((pb, one, one), (zb, one, one))) for side in FACES_Y]
    first_z = [send(side, ((pb, one, one), (zb, one, one))) for side in FACES_Z]
    for copy in loads[2]:
        copy.wait()
    later = [send(side, ((zb, two, two), (fb, one, one))) for side in CORNERS]
    later += [send(side, ((zb, rest, rest), (fb, two, two))) for side in FACES_Y + FACES_Z]

    for group in loads[3:]:
        for copy in group:
            copy.wait()

    for copy in tables:
        copy.wait()
    perm = [perm_s[i] for i in range(8)]
    stor = [stor_s[i] for i in range(8)]
    biot = [biot_s[i] for i in range(8)]
    gain = [biot_s[i] / bulk_s[i] for i in range(8)]
    coup = [biot[i] * biot[i] / bulk_s[i] for i in range(8)]
    keep = [stor[i] + coup[i] for i in range(8)]

    lane = lax.broadcasted_iota(jnp.int32, (8, LANES), 1)

    def x_up(tiles, wrap):
        rolled = [pltpu.roll(v, LANES - 1, 1) for v in tiles]
        last = lax.broadcasted_iota(jnp.int32, tiles[0].shape, 1) == LANES - 1
        out = []
        for t in range(nt):
            nxt = rolled[t + 1] if t + 1 < nt else (rolled[0] if wrap else jnp.zeros_like(rolled[0]))
            out.append(jnp.where(last, nxt, rolled[t]))
        return out

    def x_down(tiles):
        rolled = [pltpu.roll(v, 1, 1) for v in tiles]
        head = lax.broadcasted_iota(jnp.int32, tiles[0].shape, 1) == 0
        return [jnp.where(head, rolled[t - 1], rolled[t]) for t in range(nt)]

    def put_faces_x(z, start, size):
        rows = pl.ds(start, size)
        k = [kb[z, t, rows, :] for t in range(nt)]
        up = x_up(k, False)
        for t in range(nt):
            fx[z, t, rows, :] = harmonic(k[t], up[t])

    def put_faces_y(z, start, size):
        for t in range(nt):
            fy[z, t, pl.ds(start, size), :] = harmonic(
                kb[z, t, pl.ds(start, size), :], kb[z, t, pl.ds(start + 1, size), :])

    def put_faces_z(z, start, size):
        for t in range(nt):
            fz[z, t, pl.ds(start, size), :] = harmonic(
                kb[z, t, pl.ds(start, size), :], kb[z + 1, t, pl.ds(start, size), :])

    def diagonal(base, z, start, size):
        rows = pl.ds(start, size)
        low_x = x_down([fx[z, t, rows, :] for t in range(nt)])
        out = []
        for t in range(nt):
            d = base[t] + fz[z - 1, t, rows, :] + fz[z, t, rows, :]
            d = d + fy[z, t, pl.ds(start - 1, size), :] + fy[z, t, rows, :]
            out.append(d + low_x[t] + fx[z, t, rows, :])
        return out

    def around(src, z, start, size):
        rows, under, over = pl.ds(start, size), pl.ds(start - 1, size), pl.ds(start + 1, size)
        mid_v = [src[z, t, rows, :] for t in range(nt)]
        face = [fx[z, t, rows, :] for t in range(nt)]
        up = x_up(mid_v, True)
        down = x_down([face[t] * mid_v[t] for t in range(nt)])
        out = []
        for t in range(nt):
            total = fz[z - 1, t, rows, :] * src[z - 1, t, rows, :] + fz[z, t, rows, :] * src[z + 1, t, rows, :]
            total = total + fy[z, t, under, :] * src[z, t, under, :] + fy[z, t, rows, :] * src[z, t, over, :]
            out.append(total + down[t] + face[t] * up[t])
        return out

    def begin(z, start, size):
        rows, inner = pl.ds(start, size), pl.ds(start - TOP, size)
        diag = diagonal([eb[z - HALO, t, inner, :] for t in range(nt)], z, start, size)
        near_sum = around(pb, z, start, size)
        for t in range(nt):
            d = diag[t]
            c = (1.0 - fb[z, t, rows, :].astype(F32)) / d
            db[z - HALO, t, inner, :] = d
            cb[z, t, rows, :] = c
            u0[z, t, rows, :] = c * (bb[z - HALO, t, inner, :] - (d * pb[z, t, rows, :] - near_sum[t]))

    def advance(src, dst, z, start, size):
        rows = pl.ds(start, size)
        new = around(src, z, start, size)
        for t in range(nt):
            dst[z, t, rows, :] = cb[z, t, rows, :] * new[t]

    @pl.loop(0, nz)
    def _(z):
        for t in range(nt):
            s, a, c, g, k = pick(zb[z + HALO, t, own, :], (stor, biot, coup, gain, perm))
            kb[z + HALO, t, own, :] = k
            gb[z, t] = g
            eb[z, t] = s + c
            bb[z, t] = s * ob[z, t] + c * pb[z + HALO, t, own, :] - a * sb[z, t] + qb[z, t]

    @pl.loop(HALO, far)
    def _(z):
        put_faces_y(z, TOP, ny - 1)
        put_faces_x(z, TOP, ny)

    @pl.loop(HALO, far - 1)
    def _(z):
        put_faces_z(z, TOP, ny)

    @pl.loop(HALO + 1, far - 1)
    def _(z):
        begin(z, TOP + 1, ny - 2)

    receive(first_z)

    def put_perm(z, start, size, live):
        row = lax.broadcasted_iota(jnp.int32, (size, LANES), 0) + start
        inside = ((row >= TOP) | has[-1][1]) & ((row < TOP + ny) | has[1][1]) & live
        for t in range(nt):
            (k,) = pick(zb[z, t, pl.ds(start, size), :], (perm,))
            kb[z, t, pl.ds(start, size), :] = jnp.where(inside, k, 0.0)

    put_perm(HALO - 1, TOP, ny, has[-1][0])
    put_perm(far, TOP, ny, has[1][0])
    put_faces_z(HALO - 1, TOP, ny)
    put_faces_z(far - 1, TOP, ny)

    begin(HALO, TOP + 1, ny - 2)
    begin(far - 1, TOP + 1, ny - 2)
    receive(first_y)

    for z in range(HALO, far):
        put_perm(z, TOP - 1, 1, has[0][0])
        put_perm(z, TOP + ny, 1, has[0][0])
        put_faces_y(z, TOP - 1, 1)
        put_faces_y(z, TOP + ny - 1, 1)
    for z in range(HALO, far):
        begin(z, TOP, 1)
        begin(z, TOP + ny - 1, 1)

    second_corners = [send(side, ((u0, two, two),)) for side in CORNERS]
    second = [send(side, ((u0, three, three),)) for side in FACES_Y + FACES_Z]

    @pl.loop(HALO + 1, far - 1)
    def _(z):
        advance(u0, u1, z, TOP + 1, ny - 2)

    @pl.loop(HALO + 2, far - 2)
    def _(z):
        advance(u1, u2, z, TOP + 2, ny - 4)

    def fold(v):
        total = v[0:8]
        for i in range(8, v.shape[0], 8):
            total = total + v[i:i + 8]
        return total

    def early_step(z, acc):
        acc = list(acc)
        for t in range(nt):
            u = u0[z + HALO, t, own, :]
            w, s = db[z, t] * u, gb[z, t] * u
            for e, (a, b) in enumerate(((u, w), (w, w), (s, s))):
                acc[e] = acc[e] + fold(a * b)
        return tuple(acc)

    zero = jnp.zeros((8, LANES), F32)
    early = lax.fori_loop(0, nz, early_step, (zero,) * 3)

    receive(later)

    def put_scale(z, start, size):
        rows = pl.ds(start, size)
        base = [pick(zb[z, t, rows, :], (keep,))[0] for t in range(nt)]
        diag = diagonal(base, z, start, size)
        for t in range(nt):
            cb[z, t, rows, :] = (1.0 - fb[z, t, rows, :].astype(F32)) / diag[t]

    for z in range(HALO):
        put_perm(z, 5, 40, has[-1][0])
        put_perm(far + z, 5, 40, has[1][0])

    @pl.loop(HALO, far)
    def _(z):
        put_perm(z, 5, 3, has[0][0])
        put_perm(z, TOP + ny, 3, has[0][0])

    put_faces_z(0, 5, 40)
    for z in (1, 2, far, far + 1):
        put_faces_z(z, 5, 40)
        put_faces_y(z, 5, 38)
        put_faces_x(z, 5, 40)

    @pl.loop(HALO, far)
    def _(z):
        for start in (6, 40):
            put_faces_z(z, start, 2)
            put_faces_x(z, start, 2)
        put_faces_y(z, 5, 2)
        put_faces_y(z, 40, 2)

    for z in (1, 2, far, far + 1):
        put_scale(z, 6, 36)

    @pl.loop(HALO, far)
    def _(z):
        put_scale(z, 6, 2)
        put_scale(z, 40, 2)

    receive(second)
    receive(second_corners)

    for z in range(HALO + 1, far - 1):
        advance(u0, u1, z, 6, 3)
        advance(u0, u1, z, 39, 3)
    for z in (HALO, far - 1):
        advance(u0, u1, z, 6, 36)
    for z in (HALO - 1, far):
        advance(u0, u1, z, 7, 34)
    for z in (HALO - 2, far + 1):
        advance(u0, u1, z, 8, 32)

    advance(u1, u2, HALO - 1, TOP, ny)
    advance(u1, u2, far, TOP, ny)

    for z in (HALO, HALO + 1, far - 2, far - 1):
        advance(u1, u2, z, TOP - 1, ny + 2)

    for z in range(HALO + 2, far - 2):
        advance(u1, u2, z, TOP - 1, 3)
        advance(u1, u2, z, TOP + ny - 2, 3)

    def moment_step(z, acc):
        zz = z + HALO
        new = around(u2, zz, TOP, ny)
        acc = list(acc)
        for t in range(nt):
            d = db[z, t]
            last = (1.0 - fb[zz, t, own, :].astype(F32)) * new[t]
            w3[z, t] = last
            u = [u0[zz, t, own, :], u1[zz, t, own, :], u2[zz, t, own, :]]
            w = [d * v for v in u] + [last]
            for e, (i, j) in enumerate(((0, 1), (1, 1), (1, 2), (2, 2), (2, 3))):
                acc[e] = acc[e] + fold(u[i] * w[j])
        return tuple(acc)

    def norm_step(z, acc):
        zz = z + HALO
        acc = list(acc)
        for t in range(nt):
            d, g = db[z, t], gb[z, t]
            u = [u0[zz, t, own, :], u1[zz, t, own, :], u2[zz, t, own, :]]
            w = [d * v for v in u] + [w3[z, t]]
            s = [g * v for v in u]
            e = 0
            for i in range(4):
                for j in range(max(i, 1), 4):
                    acc[e] = acc[e] + fold(w[i] * w[j])
                    e += 1
            for i in range(3):
                for j in range(max(i, 1), 3):
                    acc[e] = acc[e] + fold(s[i] * s[j])
                    e += 1
        return tuple(acc)

    sub = lax.broadcasted_iota(jnp.int32, (8, LANES), 0)

    def merge(a, b, step):
        take = (sub & step) == 0
        return jnp.where(take, a, b) + pltpu.roll(jnp.where(take, b, a), step, 0)

    def in_lanes(acc):
        line = zero
        for i in range(0, len(acc), 8):
            eight = (acc[i:i + 8] + [zero] * 8)[:8]
            four = [merge(eight[j], eight[j + 1], 1) for j in range(0, 8, 2)]
            pair = [merge(four[j], four[j + 1], 2) for j in range(0, 4, 2)]
            whole = jnp.sum(merge(pair[0], pair[1], 4), axis=1, keepdims=True)
            line = line + jnp.where(lane == sub + i, whole, 0.0)
        return jnp.sum(line, axis=0, keepdims=True)

    def share(value, place, slots, rank, size, peer, out_sem, in_sem):
        lines[place] = value
        slots[rank] = value
        for j in range(1, size):
            pltpu.make_async_remote_copy(
                src_ref=lines.at[place], dst_ref=slots.at[rank], send_sem=out_sem, recv_sem=in_sem,
                device_id=peer(j), device_id_type=MESH).start()
        all_of = slots.at[pl.ds(0, size - 1)]
        return pltpu.make_async_remote_copy(
            src_ref=all_of, dst_ref=all_of, send_sem=out_sem, recv_sem=in_sem,
            device_id=peer(1), device_id_type=MESH)

    def gather(flight, slots, size):
        flight.wait_recv()
        total = [slots[j] for j in range(size)]
        while len(total) > 1:
            total = [total[j] + total[j + 1] for j in range(0, len(total), 2)]
        return total[0]

    acc = list(lax.fori_loop(0, nz // 2, lambda i, a: moment_step(2 * i + 1, moment_step(2 * i, a)), (zero,) * 5))
    acc = [early[0]] + acc
    flight_a1 = share(in_lanes(acc), 0, slots_a1, rank_a, size_a, peer_a, asem.at[0], arsem.at[0])
    acc = list(lax.fori_loop(0, nz, norm_step, (zero,) * 14))
    acc = [early[1]] + acc[:9] + [early[2]] + acc[9:]
    flight_a2 = share(in_lanes(acc), 1, slots_a2, rank_a, size_a, peer_a, asem.at[1], arsem.at[1])
    for side, units, sems in second + second_corners:
        @pl.when(exists(opposite(side)))
        def _():
            bytes_of(side, sent[side], sems).wait_send()
    part = gather(flight_a1, slots_a1, size_a)
    flight_b1 = share(part, 2, slots_b1, rank_b, size_b, peer_b, bsem.at[0], brsem.at[0])
    part = gather(flight_a2, slots_a2, size_a)
    flight_b2 = share(part, 3, slots_b2, rank_b, size_b, peer_b, bsem.at[1], brsem.at[1])
    flight_a1.wait_send()
    flight_a2.wait_send()
    total = gather(flight_b1, slots_b1, size_b)

    def at(e):
        return jnp.broadcast_to(total[:, e:e + 1], (1, LANES))

    m = [at(e) for e in range(6)]
    h = [m[i] - m[i + 1] for i in range(5)]
    l1, l2 = h[1] / h[0], h[2] / h[0]
    d1 = h[2] - l1 * h[1]
    e1 = h[3] - l1 * h[2]
    y1 = m[1] - l1 * m[0]
    ok1 = d1 > 1e-7 * h[2]
    safe1 = jnp.where(ok1, d1, 1.0)
    l3 = e1 / safe1
    d2 = h[4] - l2 * h[2] - l3 * e1
    y2 = m[2] - l2 * m[0] - l3 * y1
    ok2 = ok1 & (d2 > 1e-7 * h[4])
    c2 = jnp.where(ok2, y2 / jnp.where(ok2, d2, 1.0), 0.0)
    c1 = jnp.where(ok1, (y1 - e1 * c2) / safe1, 0.0)
    c0 = (m[0] - h[1] * c1 - h[2] * c2) / h[0]
    coef = [c0, c1, c2]

    b0, b1, b2 = [jnp.broadcast_to(v, (ny, LANES)) for v in coef]

    @pl.loop(0, nz)
    def _(z):
        zz = z + HALO
        for t in range(nt):
            delta = b0 * u0[zz, t, own, :] + b1 * u1[zz, t, own, :] + b2 * u2[zz, t, own, :]
            press_out[z, :, pl.ds(LANES * t, LANES)] = pb[zz, t, own, :] + delta
            strain_out[z, :, pl.ds(LANES * t, LANES)] = sb[z, t] + gb[z, t] * delta

    flight_b1.wait_send()
    flight_b2.wait_send()
    tail_out[0:1, :] = gather(flight_b2, slots_b2, size_b)
    for i in range(3):
        tail_out[i + 1:i + 2, :] = coef[i]


def norms(tail, cells):
    def at(e):
        return jnp.broadcast_to(tail[0:1, e:e + 1], (1, LANES))

    c = [tail[i:i + 1] for i in range(1, 4)]
    left = [1.0 - c[0], c[0] - c[1], c[1] - c[2], c[2]]
    e = 0
    out = []
    for v in (left, c):
        total = jnp.zeros((1, LANES), F32)
        for i in range(len(v)):
            for j in range(i, len(v)):
                total = total + (1.0 if i == j else 2.0) * v[i] * v[j] * at(e)
                e += 1
        out.append(total)
    lane = lax.broadcasted_iota(jnp.int32, (1, LANES), 1)
    return jnp.sqrt(jnp.maximum(jnp.where(lane == 0, out[0], out[1]), 0.0) / cells)


def solution(mesh):
    shape_z, shape_y = mesh.shape["gz"], mesh.shape["gy"]

    def per_device(zone_ids, fixed_cells, pressure_old, pressure_iter, strain_change, source,
                   zone_perm, zone_storage, zone_biot, zone_bulk):
        nz, ny, nx = zone_ids.shape
        nt = nx // LANES
        size_a = LINE * CORES
        size_b = shape_z * shape_y // size_a
        ext = (nz + 2 * HALO, nt, ny + 2 * TOP, LANES)
        inner = (nz, nt, ny, LANES)
        block = jax.ShapeDtypeStruct((nz, ny, nx), F32)
        dma = pltpu.SemaphoreType.DMA

        def kernel(*refs):
            body(shape_z, shape_y, nz, ny, nt, *refs)

        results = pl.pallas_call(
            kernel,
            out_shape=(pltpu.VMEM((nz, ny, nx), F32), pltpu.VMEM((nz, ny, nx), F32), pltpu.VMEM((8, LANES), F32)),
            in_specs=[pl.BlockSpec(memory_space=pl.ANY)] * 10,
            out_specs=tuple([pl.BlockSpec(memory_space=pltpu.VMEM)] * 3),
            scratch_shapes=[
                pltpu.VMEM(ext, jnp.int32), pltpu.VMEM(ext, jnp.int32),
            ] + [pltpu.VMEM(ext, F32)] * 9 + [pltpu.VMEM(inner, F32)] * 8 + [
                pltpu.SMEM((8,), F32), pltpu.SMEM((8,), F32), pltpu.SMEM((8,), F32), pltpu.SMEM((8,), F32),
                pltpu.VMEM((4, 1, LANES), F32),
                pltpu.VMEM((size_a, 1, LANES), F32), pltpu.VMEM((size_b, 1, LANES), F32),
                pltpu.VMEM((size_a, 1, LANES), F32), pltpu.VMEM((size_b, 1, LANES), F32),
                dma((4,)), dma((6,)), dma((8,)), dma((20,)),
                dma((2,)), dma((2,)), dma((2,)), dma((2,)),
            ],
            compiler_params=pltpu.CompilerParams(collective_id=0, has_side_effects=True),
        )(zone_ids, fixed_cells, pressure_old, pressure_iter, strain_change, source,
          zone_perm, zone_storage, zone_biot, zone_bulk)

        cells = float(nz * shape_z * ny * shape_y * nx)

        def emit(press_in, strain_in, tail_in, press_ref, strain_ref, norms_ref, pair, sem, pair_sem):
            copies = []
            for i, (a, b) in enumerate(((press_in, press_ref), (strain_in, strain_ref))):
                for j in range(4):
                    part = pl.ds(j * nz // 4, nz // 4)
                    copy = pltpu.make_async_copy(a.at[part], b.at[part], sem.at[i, j])
                    copy.start()
                    copies.append(copy)
            both = norms(tail_in[...], cells)
            pair[0] = both[0, 0]
            pair[1] = both[0, 1]
            copy = pltpu.make_async_copy(pair, norms_ref, pair_sem)
            copy.start()
            copies.append(copy)
            for copy in copies:
                copy.wait()

        return pl.pallas_call(
            emit,
            out_shape=(block, block, jax.ShapeDtypeStruct((2,), F32)),
            in_specs=[pl.BlockSpec(memory_space=pltpu.VMEM)] * 3,
            out_specs=(pl.BlockSpec(memory_space=pl.ANY),) * 3,
            scratch_shapes=[pltpu.SMEM((2,), F32), dma((2, 4)), dma],
        )(*[pltpu.with_memory_space_constraint(v, pltpu.VMEM) for v in results])

    field = P("gz", "gy", None)
    return jax.shard_map(
        per_device, mesh=mesh,
        in_specs=(field,) * 6 + (P(),) * 4,
        out_specs=(field, field, P()),
        check_vma=False,
    )
```
